256 devices in a mesh: wide: 16 (over z, core), ctx: 16 (over y, x).
Axes of the slice: x: 4, y: 4, z: 8, core: 2. Of those that a mesh axis runs over, the one named last changes fastest.
Arguments:
- residual: float32 [256, 4096], P('wide', 'ctx'), may hold values from -40 to 40
- grad_out: float32 [256, 4096], P('wide', 'ctx'), may hold values from -6 to 6
- norm_gain: float32 [4096], P('ctx'), may hold values from 0.5 to 1.5
- w_gate: float32 [4096, 14336], P('ctx', 'wide'), may hold values from -0.09375 to 0.09375
- w_up: float32 [4096, 14336], P('ctx', 'wide'), may hold values from -0.09375 to 0.09375
- w_down: float32 [14336, 4096], P('wide', 'ctx'), may hold values from -0.046875 to 0.046875
- w_out: float32 [4096, 4096], P('wide', 'ctx'), may hold values from -0.09375 to 0.09375
- queries: float32 [256, 4096], P('ctx', 'wide'), may hold values from -12 to 12
- attn_out: float32 [256, 4096], P('ctx', 'wide'), may hold values from -3 to 3
- log_sum_exp: float32 [32, 256], P('wide', 'ctx'), as said below
- key_cache: float32 [16, 16384, 128], P('wide', 'ctx'), may hold values from -16 to 16
- value_cache: float32 [16, 16384, 128], P('wide', 'ctx'), may hold values from -6 to 6
Outputs:
- grad_w_gate: float32 [4096, 14336], P('ctx', 'wide')
- grad_w_up: float32 [4096, 14336], P('ctx', 'wide')
- grad_w_down: float32 [14336, 4096], P('wide', 'ctx')
- grad_w_out: float32 [4096, 4096], P('wide', 'ctx')
- grad_resid: float32 [256, 4096], P('wide', 'ctx')
- grad_queries: float32 [256, 4096], P('ctx', 'wide')
The draws below stay inside these ranges and needn't reach their ends.
Inputs may be any that keep to these rules, and one draw needn't show every extreme that they name: `log_sum_exp`: for each head and row, the logarithm of the sum of exp(score) over the positions that the row sees, with score as in the reference program, plus a shift between 0 and 0.2.
All inputs are finite; a program needn't handle non-finite values.
Results may differ from the reference program's by a relative error of at most 0.0003.
Values sent between devices are 32-bit elements; how exact they have to be, the bound alone decides.
A program may use at most 64 MiB of HBM per device.

```python
import math
import jax
import jax.numpy as jnp
from jax import lax

D = 4096
FF = 14336
QH = 32
KVH = 8
HD = 128
ROWS = 256
SPLIT = 2
CONTEXT = 32768


def joint_draw(key):
    query_key = jax.random.fold_in(key, 101)
    cache_key = jax.random.fold_in(key, 202)
    drawn_queries = jax.random.normal(query_key, (ROWS, QH * HD), jnp.float32)
    drawn_keys = 2.0 * jax.random.normal(cache_key, (KVH * SPLIT, CONTEXT // SPLIT, HD), jnp.float32)
    return (drawn_queries, drawn_keys)


def draw_queries(key, part):
    return joint_draw(key)[0]


def draw_key_cache(key, part):
    return joint_draw(key)[1]


def draw_log_sum_exp(key, part):
    drawn_queries, drawn_keys = joint_draw(key)
    grouped = drawn_keys.reshape(KVH, CONTEXT, HD)
    query_heads = drawn_queries.reshape(ROWS, QH, HD).transpose(1, 0, 2)
    query_pos = CONTEXT - ROWS + jnp.arange(ROWS, dtype=jnp.int32)
    key_pos = jnp.arange(CONTEXT, dtype=jnp.int32)

    def one_head(head_index):
        head_keys = lax.dynamic_index_in_dim(grouped, head_index // (QH // KVH), 0, keepdims=False)
        head_queries = lax.dynamic_index_in_dim(query_heads, head_index, 0, keepdims=False)
        scores = jnp.dot(head_queries, head_keys.T, precision=lax.Precision.HIGHEST) / math.sqrt(HD)
        scores = jnp.where(key_pos[None, :] <= query_pos[:, None], scores, -1e+30)
        return jax.nn.logsumexp(scores, axis=1)
    exact = lax.map(one_head, jnp.arange(QH, dtype=jnp.int32))
    shifted = jax.random.uniform(jax.random.fold_in(key, 303), (QH, ROWS), jnp.float32, 0.0, 0.2)
    return exact + shifted


def draw_residual(key, part):
    base = jax.random.normal(jax.random.fold_in(key, 505), (ROWS, D), jnp.float32)
    rough = jax.random.uniform(jax.random.fold_in(key, 606), (ROWS, D), jnp.float32, 0.7, 1.4)
    column_scale = jnp.exp(jnp.linspace(math.log(0.6), math.log(1.8), D))
    return base * rough * column_scale[None, :]


def block_scale(rng, extent, split, low, largest):
    def one(axis_at, parts):
        steps = jax.random.uniform(jax.random.fold_in(jax.random.fold_in(rng, 6), axis_at), (parts,), jnp.float32, low / len(split), largest / len(split))
        return jnp.repeat(jnp.exp(steps), extent[axis_at] // parts).reshape((-1,) + (1,) * (len(extent) - axis_at - 1))

    factor_of = one(*split[0])
    for cut in split[1:]:
        factor_of = factor_of * one(*cut)
    return factor_of


def bell_draw(own_key, extent, scale, most, pieces=(), held_as=jnp.bfloat16):
    values = scale * jax.random.normal(own_key, extent, jnp.float32)
    if pieces:
        values = values * block_scale(own_key, extent, pieces, -0.22, 0.18)
    return jnp.clip(values, -most, most).astype(held_as)


def setup_inputs(seed: int = 0) -> dict:
    keys = jax.random.split(jax.random.key(seed), 13)
    residual = draw_residual(jax.random.fold_in(keys[12], 71), 0)
    grad_out = bell_draw(keys[1], (ROWS, D), 1.0, 6.0, ((0, 16), (1, 16)), jnp.float32)
    norm_gain = jnp.clip(1.0 + 0.1 * jax.random.normal(keys[2], (D,), jnp.float32), 0.5, 1.5)
    w_gate = bell_draw(keys[3], (D, FF), D ** -0.5, 0.09375, ((0, 16), (1, 16)), jnp.float32)
    w_up = bell_draw(keys[4], (D, FF), D ** -0.5, 0.09375, ((0, 16), (1, 16)), jnp.float32)
    w_down = bell_draw(keys[5], (FF, D), FF ** -0.5, 0.046875, ((0, 16), (1, 16)), jnp.float32)
    w_out = bell_draw(keys[6], (QH * HD, D), D ** -0.5, 0.09375, ((0, 16), (1, 16)), jnp.float32)
    queries = draw_queries(jax.random.fold_in(keys[12], 71), 0)
    attn_out = bell_draw(keys[8], (ROWS, QH * HD), 0.5, 3.0, ((0, 16), (1, 16)), jnp.float32)
    log_sum_exp = draw_log_sum_exp(jax.random.fold_in(keys[12], 71), 0)
    key_cache = draw_key_cache(jax.random.fold_in(keys[12], 71), 0)
    value_cache = bell_draw(keys[11], (KVH * SPLIT, CONTEXT // SPLIT, HD), 1.0, 6.0, ((0, 16), (1, 16)), jnp.float32)
    return {"residual": residual, "grad_out": grad_out, "norm_gain": norm_gain, "w_gate": w_gate, "w_up": w_up, "w_down": w_down, "w_out": w_out, "queries": queries, "attn_out": attn_out, "log_sum_exp": log_sum_exp, "key_cache": key_cache, "value_cache": value_cache}


epsilon = 1e-05
highest = lax.Precision.HIGHEST

def matmul(left, right):
    return jnp.dot(left, right, precision=highest, preferred_element_type=jnp.float32)

def reference(residual, grad_out, norm_gain, w_gate, w_up, w_down, w_out, queries, attn_out, log_sum_exp, key_cache, value_cache):
    inv_rms = lax.rsqrt(lax.optimization_barrier(jnp.mean(residual * residual, axis=1)) + epsilon)
    normed = residual * inv_rms[:, None] * norm_gain[None, :]
    gate_out = matmul(normed, w_gate)
    up_out = matmul(normed, w_up)
    d_hidden = matmul(grad_out, w_down.T)
    sigmoid_gate = jax.nn.sigmoid(gate_out)
    activated = gate_out * sigmoid_gate
    hidden = activated * up_out
    grad_w_down = matmul(hidden.T, grad_out)
    d_up = d_hidden * activated
    d_gate = d_hidden * up_out * sigmoid_gate * (1.0 + gate_out * (1.0 - sigmoid_gate))
    grad_w_gate = matmul(normed.T, d_gate)
    grad_w_up = matmul(normed.T, d_up)
    d_normed = matmul(d_gate, w_gate.T) + matmul(d_up, w_up.T)
    scaled = d_normed * norm_gain[None, :]
    row_dot = lax.optimization_barrier(jnp.sum(residual * scaled, axis=1))
    cubed = inv_rms * inv_rms * inv_rms
    grad_resid = grad_out + inv_rms[:, None] * scaled - residual * (cubed * row_dot / D)[:, None]
    d_attn = matmul(grad_resid, w_out.T)
    grad_w_out = matmul(attn_out.T, grad_resid)
    all_keys = key_cache.reshape(KVH, CONTEXT, HD)
    all_values = value_cache.reshape(KVH, CONTEXT, HD)
    query_heads = queries.reshape(ROWS, QH, HD).transpose(1, 0, 2)
    dout_heads = d_attn.reshape(ROWS, QH, HD).transpose(1, 0, 2)
    output_heads = attn_out.reshape(ROWS, QH, HD).transpose(1, 0, 2)
    delta = lax.optimization_barrier(jnp.sum(dout_heads * output_heads, axis=2))
    scale = 1.0 / HD ** 0.5
    query_pos = CONTEXT - ROWS + jnp.arange(ROWS, dtype=jnp.int32)
    key_pos = jnp.arange(CONTEXT, dtype=jnp.int32)
    visible = key_pos[None, :] <= query_pos[:, None]

    def one_head(head_index):
        group_index = head_index // (QH // KVH)
        head_keys = lax.dynamic_index_in_dim(all_keys, group_index, 0, keepdims=False)
        head_values = lax.dynamic_index_in_dim(all_values, group_index, 0, keepdims=False)
        head_queries = lax.dynamic_index_in_dim(query_heads, head_index, 0, keepdims=False)
        head_dout = lax.dynamic_index_in_dim(dout_heads, head_index, 0, keepdims=False)
        head_lse = lax.dynamic_index_in_dim(log_sum_exp, head_index, 0, keepdims=False)
        head_delta = lax.dynamic_index_in_dim(delta, head_index, 0, keepdims=False)
        scores = matmul(head_queries, head_keys.T) * scale
        probs = jnp.where(visible, jnp.exp(scores - head_lse[:, None]), 0.0)
        dprobs = matmul(head_dout, head_values.T)
        return matmul(probs * (dprobs - head_delta[:, None]), head_keys) * scale
    per_head = lax.map(one_head, jnp.arange(QH, dtype=jnp.int32))
    grad_queries = per_head.transpose(1, 0, 2).reshape(ROWS, QH * HD)
    return (grad_w_gate, grad_w_up, grad_w_down, grad_w_out, grad_resid, grad_queries)
```

```python
import math

import jax
import jax.numpy as jnp
from jax import lax
from jax.experimental import pallas as pl
from jax.experimental.pallas import tpu as pltpu
from jax.sharding import Mesh
from jax.sharding import PartitionSpec as P

MESH = pl.DeviceIdType.MESH
F32 = jnp.float32
BF16 = jnp.bfloat16
EPS = 1e-05
NZ, NX, NY = 8, 4, 4
NCTX = NX * NY
OFF = (0, 1, -1, 2, -2, 3, -3, 4)
SLOT = {o: s for s, o in enumerate(OFF)}
D, FF, HD = 4096, 14336, 128
WD, WF = D // NCTX, FF // 16
ROWS, BR = 256, 16
HALF = 11 * 128
WIDTH = 2 * HALF
KEYS = 1024
CONTEXT = 32768
SCALE = 1.0 / math.sqrt(HD)


def split(v):
    hi = v.astype(BF16)
    return hi, (v - hi.astype(F32)).astype(BF16)


def nn(a, b):
    return lax.dot_general(a, b, (((1,), (0,)), ((), ())), preferred_element_type=F32)


def nt(a, b):
    return lax.dot_general(a, b, (((1,), (1,)), ((), ())), preferred_element_type=F32)


def three(a, bh, bl, dot):
    ah, al = split(a)
    m = a.shape[0]
    both = dot(jnp.concatenate([ah, al], axis=0), bh)
    return both[:m] + both[m:] + dot(ah, bl)


def kernel(
    resid_h, grad_h, gain_h, wg_h, wu_h, wd_h, wo_h, qol_h, key_h, val_h,
    gwg_o, gwu_o, gwd_o, gwo_o, gres_o, gq_o,
    rg, gain, w2f, wdf, wof, w2h, w2l, wdh, wdl, woh, wol, qol, kv, k3, v3,
    part, r1, d1, c1, q1, r2, d2, c2, full, tpart, tpair, usum, rz, gres, da, rda, dat,
    probs, acc, dq, rdq, gw2, gwd, gwo, gqs,
    lsem, ssem, rsem,
):
    z, core = lax.axis_index("z"), lax.axis_index("core")
    y, x = lax.axis_index("y"), lax.axis_index("x")
    me = y * NX + x
    other = 1 - core
    wide = 2 * z + core

    counter = {"l": 0, "r": 0}
    started = []

    def local(src, dst):
        copy = pltpu.make_async_copy(src, dst, lsem.at[counter["l"]])
        counter["l"] += 1
        copy.start()
        return copy

    def send(src, dst, dev):
        n = counter["r"]
        counter["r"] += 1
        copy = pltpu.make_async_remote_copy(
            src_ref=src, dst_ref=dst, send_sem=ssem.at[n], recv_sem=rsem.at[n],
            device_id=dev, device_id_type=MESH,
        )
        copy.start()
        started.append(copy)
        return copy

    def at_z(o):
        return {"z": lax.rem(z + (o + NZ), NZ)}

    def at_x(o):
        return {"x": lax.rem(x + (o + NX), NX)}

    def at_y(o):
        return {"y": lax.rem(y + (o + NY), NY)}

    pair = {"core": other}
    ctx_offsets = sorted(
        [(dy, dx) for dy in range(NY) for dx in range(NX) if (dy, dx) != (0, 0)],
        key=lambda o: -(min(o[0], 4 - o[0]) + min(o[1], 4 - o[1])),
    )

    def at_ctx(dy, dx):
        return {"y": lax.rem(y + dy, NY), "x": lax.rem(x + dx, NX)}

    def ctx_of(dy, dx):
        return lax.rem(y + dy, NY) * NX + lax.rem(x + dx, NX)

    l_rg = [local(resid_h, rg.at[0, core, 0]), local(grad_h, rg.at[0, core, 1])]
    l_qol = local(qol_h, qol.at[me])
    l_gain = local(gain_h, gain)
    l_w = [local(wg_h, w2f.at[0]), local(wu_h, w2f.at[1]), local(wd_h, wdf), local(wo_h, wof)]
    l_kv = [local(key_h.at[0], kv.at[0, core]), local(val_h.at[0], kv.at[1, core])]

    barrier = pltpu.get_barrier_semaphore()
    peers = [pair] + [at_z(o) for o in OFF[1:]] + [at_ctx(*o) for o in ctx_offsets]
    for dev in peers:
        pl.semaphore_signal(barrier, inc=1, device_id=dev, device_id_type=MESH)
    pl.semaphore_wait(barrier, len(peers))

    for c in l_rg:
        c.wait()
    zp, zm, pr = {}, {}, {}

    def zsend(bag, o, s_from, s_to, sub=None):
        a = rg.at[s_from, core] if sub is None else rg.at[s_from, core, sub]
        b = rg.at[s_to, core] if sub is None else rg.at[s_to, core, sub]
        bag[s_to] = send(a, b, at_z(o))

    def psend(s):
        pr[s] = send(rg.at[s, core], rg.at[s, core], pair)

    zsend(zp, 1, 0, SLOT[-1])
    zsend(zm, -1, 0, SLOT[1])
    psend(0)
    l_qol.wait()
    qo_in = [send(qol.at[me], qol.at[me], at_ctx(*o)) for o in ctx_offsets]
    kv_in = [send(key_h.at[0], kv.at[0, core], pair), send(val_h.at[0], kv.at[1, core], pair)]

    for c in l_w:
        c.wait()
    l_gain.wait()

    @pl.loop(0, WD // 32)
    def _(i):
        rows = pl.ds(pl.multiple_of(i * 32, 32), 32)
        for n in range(2):
            hi, lo = split(w2f[n, rows, :])
            w2h[rows, n * WF : (n + 1) * WF] = hi
            w2l[rows, n * WF : (n + 1) * WF] = lo
        hi, lo = split(wof[rows, :])
        woh[rows, :] = hi
        wol[rows, :] = lo

    @pl.loop(0, WF // 128)
    def _(i):
        rows = pl.ds(pl.multiple_of(i * 128, 128), 128)
        hi, lo = split(wdf[rows, :])
        wdh[rows, :] = hi
        wdl[rows, :] = lo

    zp[SLOT[-1]].wait_recv()
    zsend(zp, 1, SLOT[-1], SLOT[-2])
    psend(SLOT[-1])
    zm[SLOT[1]].wait_recv()
    zsend(zm, -1, SLOT[1], SLOT[2])
    psend(SLOT[1])
    zm[SLOT[2]].wait_recv()
    zsend(zm, -1, SLOT[2], SLOT[3])
    psend(SLOT[2])
    zp[SLOT[-2]].wait_recv()
    zsend(zp, 1, SLOT[-2], SLOT[-3])
    psend(SLOT[-2])

    def project(k):
        both = rg[4 * k : 4 * k + 4]
        resid = both[:, :, 0].reshape(128, WD)
        grad = both[:, :, 1].reshape(128, WD)
        squares = jnp.sum(resid * resid, axis=1, keepdims=True)
        part[k, :, :, :, 2688:] = jnp.broadcast_to(squares, (128, 128)).reshape(4, 4, 8, 128)
        xh, xl = split(resid * gain[...])
        xx = jnp.concatenate([xh, xl], axis=0)
        for n in range(7):
            cols = slice(n * 256, (n + 1) * 256)
            two = nn(xx, w2h[:, cols])
            part[k, :, :, :, cols] = (two[:128] + two[128:] + nn(xh, w2l[:, cols])).reshape(4, 4, 8, 256)
        gh, gl = split(grad)
        gg = jnp.concatenate([gh, gl], axis=0)
        for lo, hi in ((0, 256), (256, 512), (512, 768), (768, 896)):
            two = nt(gg, wdh[lo:hi, :])
            part[k, :, :, :, 1792 + lo : 1792 + hi] = (
                two[:128] + two[128:] + nt(gh, wdl[lo:hi, :])
            ).reshape(4, 4, 8, hi - lo)

    axes = ((at_x, x, at_y, y), (at_y, y, at_x, x))
    cs = (slice(0, HALF), slice(HALF, WIDTH))
    LO, HI = slice(0, 640), slice(640, HALF)

    def wrap(v, o):
        return lax.rem(v + (o + 4), 4)

    def pview(ref, k, h, b, a):
        return ref.at[k, b, a, :, cs[h]] if h == 0 else ref.at[k, a, b, :, cs[h]]

    def pread(ref, k, h, b, a):
        return ref[k, b, a, :, cs[h]] if h == 0 else ref[k, a, b, :, cs[h]]

    B01, B23 = pl.ds(0, 2), pl.ds(2, 2)
    m1, m2 = {}, {}

    def rs1_send(k):
        for h in range(2):
            go, av, _, _ = axes[h]
            m1[k, h, "rp"] = send(pview(part, k, h, B01, wrap(av, 2)), r1.at[k, h, 0], go(1))
            m1[k, h, "rm"] = send(pview(part, k, h, B23, wrap(av, 2)), r1.at[k, h, 1], go(-1))
        for h in range(2):
            go, av, _, _ = axes[h]
            m1[k, h, "dp"] = send(pview(part, k, h, B23, wrap(av, 1)), d1.at[k, h, 0], go(1))
            m1[k, h, "dm"] = send(pview(part, k, h, B01, wrap(av, -1)), d1.at[k, h, 1], go(-1))

    def rs1_relay(k):
        for h in range(2):
            go, av, _, _ = axes[h]
            m1[k, h, "rp"].wait_recv()
            r1[k, h, 0] = r1[k, h, 0] + pread(part, k, h, B01, wrap(av, 1))
            m1[k, h, "cp"] = send(r1.at[k, h, 0], c1.at[k, h, 0], go(1))
            m1[k, h, "rm"].wait_recv()
            r1[k, h, 1] = r1[k, h, 1] + pread(part, k, h, B23, wrap(av, -1))
            m1[k, h, "cm"] = send(r1.at[k, h, 1], c1.at[k, h, 1], go(-1))

    def rs1_final(k):
        for h in range(2):
            _, av, go, bv = axes[h]
            for n in ("dp", "dm", "cp", "cm"):
                m1[k, h, n].wait_recv()
            q1[k, h, 0:2] = pread(part, k, h, B01, av) + c1[k, h, 0] + d1[k, h, 1]
            q1[k, h, 2:4] = pread(part, k, h, B23, av) + d1[k, h, 0] + c1[k, h, 1]
            m2[k, h, "rp"] = send(q1.at[k, h, wrap(bv, 2), :, LO], r2.at[k, h, 0, :, LO], go(1))
            m2[k, h, "rm"] = send(q1.at[k, h, wrap(bv, 2), :, HI], r2.at[k, h, 1, :, HI], go(-1))
            m2[k, h, "dp"] = send(q1.at[k, h, wrap(bv, 1), :, HI], d2.at[k, h, 0, :, HI], go(1))
            m2[k, h, "dm"] = send(q1.at[k, h, wrap(bv, -1), :, LO], d2.at[k, h, 1, :, LO], go(-1))

    def rs2_relay(k):
        for h in range(2):
            _, _, go, bv = axes[h]
            m2[k, h, "rp"].wait_recv()
            r2[k, h, 0, :, LO] = r2[k, h, 0, :, LO] + q1[k, h, wrap(bv, 1), :, LO]
            m2[k, h, "cp"] = send(r2.at[k, h, 0, :, LO], c2.at[k, h, 0, :, LO], go(1))
            m2[k, h, "rm"].wait_recv()
            r2[k, h, 1, :, HI] = r2[k, h, 1, :, HI] + q1[k, h, wrap(bv, -1), :, HI]
            m2[k, h, "cm"] = send(r2.at[k, h, 1, :, HI], c2.at[k, h, 1, :, HI], go(-1))

    def gate(k):
        sums = []
        for h in range(2):
            _, _, _, bv = axes[h]
            for n in ("dp", "dm", "cp", "cm"):
                m2[k, h, n].wait_recv()
            sums.append(q1[k, h, bv, :, LO] + c2[k, h, 0, :, LO] + d2[k, h, 1, :, LO])
            sums.append(q1[k, h, bv, :, HI] + d2[k, h, 0, :, HI] + c2[k, h, 1, :, HI])
        total = jnp.concatenate(sums, axis=1)
        inv = lax.rsqrt(total[:, 2688:] / D + EPS)
        inv1 = inv[:, 0:1]
        gate_raw, up_raw, d_hidden = total[:, 0:896], total[:, 896:1792], total[:, 1792:2688]
        gate_out, up_out = gate_raw * inv1, up_raw * inv1
        sig = jax.nn.sigmoid(gate_out)
        activated = gate_out * sig
        d_up = d_hidden * activated
        d_gate = d_hidden * up_out * sig * (1.0 + gate_out * (1.0 - sig))
        dot = jnp.sum(d_gate * gate_raw + d_up * up_raw, axis=1, keepdims=True)
        coef = inv * inv * inv * dot / D
        lane = lax.broadcasted_iota(jnp.int32, (8, 128), 1)
        full[k, y, x, :, 0:896] = activated * up_out
        full[k, y, x, :, 896:1792] = d_gate
        full[k, y, x, :, 1792:2688] = d_up
        full[k, y, x, :, 2688:] = jnp.where(lane < 64, inv, coef)

    def sub(c, part_of):
        return slice(c.start + part_of.start, c.start + part_of.stop)

    def fview(k, h, b, a, cols=None):
        cols = cs[h] if cols is None else sub(cs[h], cols)
        return full.at[k, b, a, :, cols] if h == 0 else full.at[k, a, b, :, cols]

    def fsend(bag, name, k, h, b, a, dev, cols=None):
        v = fview(k, h, b, a, cols)
        bag[k, h, name] = send(v, v, dev)

    g1, g2 = {}, {}

    def ag1_send(k):
        for h in range(2):
            _, av, go, bv = axes[h]
            fsend(g1, "p", k, h, bv, av, go(1))
            fsend(g1, "m", k, h, bv, av, go(-1))

    def ag1_relay(k):
        for h in range(2):
            _, av, go, bv = axes[h]
            g1[k, h, "p"].wait_recv()
            fsend(g1, "fp", k, h, wrap(bv, -1), av, go(1), LO)
            g1[k, h, "m"].wait_recv()
            fsend(g1, "fm", k, h, wrap(bv, 1), av, go(-1), HI)

    ALL = pl.ds(0, 4)

    def ag2_send(k):
        for h in range(2):
            go, av, _, _ = axes[h]
            g1[k, h, "fp"].wait_recv()
            g1[k, h, "fm"].wait_recv()
            fsend(g2, "p", k, h, ALL, av, go(1))
            fsend(g2, "m", k, h, ALL, av, go(-1))

    def ag2_relay(k):
        for h in range(2):
            go, av, _, _ = axes[h]
            g2[k, h, "p"].wait_recv()
            fsend(g2, "fp", k, h, B01, wrap(av, -1), go(1))
            g2[k, h, "m"].wait_recv()
            fsend(g2, "fm", k, h, B23, wrap(av, 1), go(-1))

    zf = {}
    pf = {}

    def input_grad(k):
        for h in range(2):
            g2[k, h, "fp"].wait_recv()
            g2[k, h, "fm"].wait_recv()
        dgu = full[k, :, :, :, 896:2688].reshape(128, 1792)
        tile = full[k, :, :, :, 2688:].reshape(128, 128)
        inv, coef = tile[:, 0:1], tile[:, 64:65]
        dn = three(dgu, w2h[...], w2l[...], nt)
        resid = rg[4 * k : 4 * k + 4, :, 0].reshape(128, WD)
        t = dn * gain[...] * inv - resid * coef
        tpart[k] = t.reshape(4, 2, BR, WD)
        pf[k] = send(tpart.at[k, :, other], tpair.at[k], pair)

    def input_grad_send(k):
        pf[k].wait_recv()
        usum[k] = tpart[k, :, core] + tpair[k]
        for s in range(4 * k + 3, max(4 * k, 1) - 1, -1):
            zf[s] = send(usum.at[k, s % 4], rz.at[s], at_z(OFF[s]))

    def weight_grads():
        inv = full[:, :, :, :, 2688:].reshape(ROWS, 128)[:, 0:1]
        both = rg[...]
        resid = both[:, :, 0].reshape(ROWS, WD)
        grad = both[:, :, 1].reshape(ROWS, WD)
        nt_ = (resid * gain[...] * inv).T
        nh, nl = split(nt_)
        nn2 = jnp.concatenate([nh, nl], axis=0)
        for n in range(7):
            cols = slice(896 + n * 256, 896 + (n + 1) * 256)
            bh, bl = split(full[:, :, :, :, cols].reshape(ROWS, 256))
            two = nn(nn2, bh)
            gw2[:, n * 256 : (n + 1) * 256] = two[:WD] + two[WD:] + nn(nh, bl)
        gh, gl = split(grad)
        for n in range(7):
            cols = slice(n * 128, (n + 1) * 128)
            ht = full[:, :, :, :, cols].reshape(ROWS, 128).T
            hh, hl = split(ht)
            two = nn(jnp.concatenate([hh, hl], axis=0), gh)
            gwd[cols, :] = two[:128] + two[128:] + nn(hh, gl)

    def attention_split():
        for c in l_kv:
            c.wait()
        for c in kv_in:
            c.wait_recv()

        @pl.loop(0, 16)
        def _(i):
            m, j = i // 8, lax.rem(i, 8)
            src = pl.ds(pl.multiple_of(j * 128, 128), 128)
            dst = pl.ds(pl.multiple_of(i * 128, 128), 128)
            for n, out in ((0, k3), (1, v3)):
                hi, lo = split(kv[n, m, src, :])
                out[dst, 0:128] = hi
                out[dst, 128:256] = lo
                out[dst, 256:384] = hi

    def attention_probs(h):
        q = qol[:, :, h * HD : (h + 1) * HD].reshape(ROWS, HD)
        lse = qol[:, :, 512:].reshape(ROWS, 128)[:, h : h + 1]
        qh, ql = split(q)
        q3 = jnp.concatenate([qh, qh, ql], axis=1)

        @pl.loop(0, 4)
        def _(i):
            keys = pl.ds(pl.multiple_of(i * 512, 512), 512)
            s = nt(q3, k3[keys, :]) * SCALE
            first = (i // 2) * (KEYS * NCTX) + me * KEYS + lax.rem(i, 2) * 512
            pos = first + lax.broadcasted_iota(jnp.int32, (ROWS, 512), 1)
            row = (CONTEXT - ROWS) + lax.broadcasted_iota(jnp.int32, (ROWS, 512), 0)
            probs[h, :, keys] = jnp.where(pos <= row, jnp.exp(s - lse), 0.0)

    def project_first():
        for s in (0, 1, 2, 3):
            pr[s].wait_recv()
        project(0)
        rs1_send(0)

    project_first()
    zm[SLOT[3]].wait_recv()
    zsend(zm, -1, SLOT[3], SLOT[4], 1)
    psend(SLOT[3])
    zp[SLOT[-3]].wait_recv()
    zsend(zp, 1, SLOT[-3], SLOT[4], 0)
    psend(SLOT[-3])
    zm[SLOT[4]].wait_recv()
    zp[SLOT[4]].wait_recv()
    psend(SLOT[4])
    for s in (4, 5, 6, 7):
        pr[s].wait_recv()
    project(1)
    rs1_send(1)
    rs1_relay(0)
    attention_split()
    rs1_relay(1)
    rs1_final(0)
    for c in qo_in:
        c.wait_recv()
    attention_probs(0)
    rs1_final(1)
    rs2_relay(0)
    attention_probs(1)
    rs2_relay(1)
    gate(0)
    ag1_send(0)
    gate(1)
    ag1_send(1)
    ag1_relay(0)
    ag1_relay(1)
    ag2_send(0)
    ag2_send(1)
    ag2_relay(0)
    ag2_relay(1)
    input_grad(0)
    input_grad_send(0)
    input_grad(1)
    input_grad_send(1)
    weight_grads()
    outs = [
        local(gw2.at[:, 0:WF], gwg_o),
        local(gw2.at[:, WF : 2 * WF], gwu_o),
        local(gwd, gwd_o),
    ]

    total = rg[0, core, 1] + usum[0, 0]
    for s in range(1, 8):
        zf[s].wait_recv()
        total = total + rz[s]
    gres[wide] = total
    outs.append(local(gres.at[wide], gres_o))
    gz = {}
    for s in range(7, 0, -1):
        gz[s] = send(gres.at[wide], gres.at[wide], at_z(OFF[s]))
    gp = [send(gres.at[wide], gres.at[wide], pair)]
    for s in range(1, 8):
        gz[s].wait_recv()
        w = 2 * lax.rem(z + (NZ - OFF[s]), NZ) + core
        gp.append(send(gres.at[w], gres.at[w], pair))
    for c in gp:
        c.wait_recv()

    all_gres = gres[...].reshape(ROWS, WD)
    da[...] = three(all_gres, woh[...], wol[...], nt).reshape(16, BR, WD)
    sent = []
    for n, o in enumerate(ctx_offsets):
        sent.append(send(da.at[ctx_of(*o)], rda.at[n], at_ctx(*o)))

    ot = qol[:, :, 256:512].reshape(ROWS, WD).T
    oh, ol = split(ot)
    eh, el = split(all_gres)
    two = nn(jnp.concatenate([oh, ol], axis=0), eh)
    gwo[...] = two[:WD] + two[WD:] + nn(oh, el)
    outs.append(local(gwo, gwo_o))

    own = da[me]
    for n, c in enumerate(sent):
        c.wait_recv()
        own = own + rda[n]
    dat[me] = own
    gat = [send(dat.at[me], dat.at[me], at_ctx(*o)) for o in ctx_offsets]
    for c in gat:
        c.wait_recv()

    for h in range(2):
        d_attn = dat[:, :, h * HD : (h + 1) * HD].reshape(ROWS, HD)
        o = qol[:, :, 256 + h * HD : 256 + (h + 1) * HD].reshape(ROWS, HD)
        delta = jnp.sum(d_attn * o, axis=1, keepdims=True)
        dh, dl = split(d_attn)
        d3 = jnp.concatenate([dh, dh, dl], axis=1)
        acc[...] = jnp.zeros_like(acc)

        @pl.loop(0, 4)
        def _(i):
            keys = pl.ds(pl.multiple_of(i * 512, 512), 512)
            g = probs[h, :, keys] * (nt(d3, v3[keys, :]) - delta)
            gh, gl = split(g)
            acc[...] += nn(jnp.concatenate([gh, gl], axis=0), k3[keys, 0:256])

        a = acc[...]
        out = (a[:ROWS, :HD] + a[:ROWS, HD:] + a[ROWS:, :HD] + a[ROWS:, HD:]) * SCALE
        dq[:, :, h * HD : (h + 1) * HD] = out.reshape(16, BR, HD)

    last = []
    for n, o in enumerate(ctx_offsets):
        last.append(send(dq.at[ctx_of(*o)], rdq.at[n], at_ctx(*o)))
    own = dq[me]
    for n, c in enumerate(last):
        c.wait_recv()
        own = own + rdq[n]
    gqs[...] = own
    outs.append(local(gqs, gq_o))
    for c in started:
        c.wait_send()
    for c in outs:
        c.wait()


def shards(residual, grad_out, norm_gain, w_gate, w_up, w_down, w_out, queries, attn_out, log_sum_exp, key_cache, value_cache):
    lse = jnp.pad(log_sum_exp.T, ((0, 0), (0, 126)))
    qol = jnp.concatenate([queries, attn_out, lse], axis=1)
    V = pltpu.VMEM
    shape = jax.ShapeDtypeStruct
    scratch = [
        V((8, 2, 2, BR, WD), F32),
        V((1, WD), F32),
        V((2, WD, WF), F32), V((WF, WD), F32), V((WD, WD), F32),
        V((WD, 2 * WF), BF16), V((WD, 2 * WF), BF16),
        V((WF, WD), BF16), V((WF, WD), BF16),
        V((WD, WD), BF16), V((WD, WD), BF16),
        V((16, BR, 640), F32),
        V((2, 2, KEYS, HD), F32),
        V((2 * KEYS, 384), BF16), V((2 * KEYS, 384), BF16),
        V((2, 4, 4, 8, WIDTH), F32),
        V((2, 2, 2, 2, 8, HALF), F32), V((2, 2, 2, 2, 8, HALF), F32), V((2, 2, 2, 2, 8, HALF), F32),
        V((2, 2, 4, 8, HALF), F32),
        V((2, 2, 2, 8, HALF), F32), V((2, 2, 2, 8, HALF), F32), V((2, 2, 2, 8, HALF), F32),
        V((2, 4, 4, 8, WIDTH), F32),
        V((2, 4, 2, BR, WD), F32), V((2, 4, BR, WD), F32), V((2, 4, BR, WD), F32),
        V((8, BR, WD), F32),
        V((16, BR, WD), F32), V((16, BR, WD), F32), V((15, BR, WD), F32), V((16, BR, WD), F32),
        V((2, ROWS, 2 * KEYS), F32),
        V((2 * ROWS, 2 * HD), F32),
        V((16, BR, WD), F32), V((15, BR, WD), F32),
        V((WD, 2 * WF), F32), V((WF, WD), F32), V((WD, WD), F32), V((BR, WD), F32),
        pltpu.SemaphoreType.DMA((24,)),
        pltpu.SemaphoreType.DMA((192,)),
        pltpu.SemaphoreType.DMA((192,)),
    ]
    anyspec = pl.BlockSpec(memory_space=pl.ANY)
    return pl.pallas_call(
        kernel,
        out_shape=(
            shape((WD, WF), F32), shape((WD, WF), F32), shape((WF, WD), F32),
            shape((WD, WD), F32), shape((BR, WD), F32), shape((BR, WD), F32),
        ),
        in_specs=[anyspec] * 10,
        out_specs=(anyspec,) * 6,
        scratch_shapes=scratch,
        compiler_params=pltpu.CompilerParams(
            collective_id=0, has_side_effects=True, vmem_limit_bytes=60 * 1024 * 1024
        ),
    )(residual, grad_out, norm_gain.reshape(1, WD), w_gate, w_up, w_down, w_out, qol, key_cache, value_cache)


def solution(mesh):
    torus = Mesh(mesh.devices.reshape(NZ, 2, NY, NX), ("z", "core", "y", "x"))
    wide, ctx = ("z", "core"), ("y", "x")
    return jax.shard_map(
        shards,
        mesh=torus,
        in_specs=(
            P(wide, ctx), P(wide, ctx), P(ctx), P(ctx, wide), P(ctx, wide), P(wide, ctx), P(wide, ctx),
            P(ctx, wide), P(ctx, wide), P(wide, ctx), P(wide, ctx, None), P(wide, ctx, None),
        ),
        out_specs=(P(ctx, wide), P(ctx, wide), P(wide, ctx), P(wide, ctx), P(wide, ctx), P(ctx, wide)),
        check_vma=False,
    )
```

```python
import math

import jax
import jax.numpy as jnp
from jax import lax
from jax.experimental import pallas as pl
from jax.experimental.pallas import tpu as pltpu
from jax.sharding import Mesh
from jax.sharding import PartitionSpec as P

MESH = pl.DeviceIdType.MESH
F32 = jnp.float32
BF16 = jnp.bfloat16
EPS = 1e-05
NZ, NX, NY = 8, 4, 4
NCTX = NX * NY
OFF = (0, 1, -1, 2, -2, 3, -3, 4)
SLOT = {o: s for s, o in enumerate(OFF)}
D, FF, HD = 4096, 14336, 128
WD, WF = D // NCTX, FF // 16
ROWS, BR = 256, 16
HALF = 11 * 128
WIDTH = 2 * HALF
KEYS = 1024
LIMIT = 48 * 1024 * 1024
CONTEXT = 32768
SCALE = 1.0 / math.sqrt(HD)


def split(v):
    hi = v.astype(BF16)
    return hi, (v - hi.astype(F32)).astype(BF16)


def nn(a, b):
    return lax.dot_general(a, b, (((1,), (0,)), ((), ())), preferred_element_type=F32)


def nt(a, b):
    return lax.dot_general(a, b, (((1,), (1,)), ((), ())), preferred_element_type=F32)


def three(a, bh, bl, dot):
    ah, al = split(a)
    m = a.shape[0]
    both = dot(jnp.concatenate([ah, al], axis=0), bh)
    return both[:m] + both[m:] + dot(ah, bl)


def kernel(
    resid_h, grad_h, gain_h, wg_h, wu_h, wd_h, wo_h, q_h, o_h, lse_h, key_h, val_h,
    gwg_o, gwu_o, gwd_o, gwo_o, gres_o, gq_o,
    rg, gain, lse_v, w2f, wdf, wof, w2h, w2l, wdh, wdl, woh, wol, qol, kv, k3, v3,
    part, r1, c1, q1, r2, c2, full, tpart, tpair, usum, rz, gres, da, rda, dat,
    probs, acc, dq, rdq, gw2, gwd, gwo, gqs,
    lsem, ssem, rsem,
):
    z, core = lax.axis_index("z"), lax.axis_index("core")
    y, x = lax.axis_index("y"), lax.axis_index("x")
    me = y * NX + x
    other = 1 - core
    wide = 2 * z + core

    counter = {"l": 0}
    out_at, in_at = {}, {}

    def local(src, dst):
        copy = pltpu.make_async_copy(src, dst, lsem.at[counter["l"]])
        counter["l"] += 1
        copy.start()
        return copy

    def transfer(src, dst, out, into, dev):
        return pltpu.make_async_remote_copy(
            src_ref=src, dst_ref=dst,
            send_sem=ssem.at[out_at.setdefault(out, len(out_at))],
            recv_sem=rsem.at[in_at.setdefault(into, len(in_at))],
            device_id=dev, device_id_type=MESH,
        )

    def send(src, dst, dev, out, into):
        copy = transfer(src, dst, out, into, dev)
        copy.start()
        return copy

    def arrived(into, like):
        transfer(like, like, next(iter(out_at)), into, pair).wait_recv()

    def gone(out, like):
        transfer(like, like, out, next(iter(in_at)), pair).wait_send()

    def at_z(o):
        return {"z": lax.rem(z + (o + NZ), NZ)}

    def at_x(o):
        return {"x": lax.rem(x + (o + NX), NX)}

    def at_y(o):
        return {"y": lax.rem(y + (o + NY), NY)}

    pair = {"core": other}
    ctx_offsets = sorted(
        [(dy, dx) for dy in range(NY) for dx in range(NX) if (dy, dx) != (0, 0)],
        key=lambda o: -(min(o[0], 4 - o[0]) + min(o[1], 4 - o[1])),
    )

    def at_ctx(dy, dx):
        return {"y": lax.rem(y + dy, NY), "x": lax.rem(x + dx, NX)}

    def ctx_of(dy, dx):
        return lax.rem(y + dy, NY) * NX + lax.rem(x + dx, NX)

    l_rg = [local(resid_h, rg.at[0, core, 0]), local(grad_h, rg.at[0, core, 1])]
    l_lse = local(lse_h, lse_v)
    l_w = [local(wg_h, w2f.at[0]), local(wu_h, w2f.at[1])]
    l_wd = [local(wd_h, wdf), local(wo_h, wof), local(gain_h, gain)]
    l_qol = [local(q_h, qol.at[me, :, 0:256]), local(o_h, qol.at[me, :, 256:512])]
    l_kv = [local(key_h.at[0], kv.at[0, core]), local(val_h.at[0], kv.at[1, core])]

    barrier = pltpu.get_barrier_semaphore()
    peers = [pair] + [go(o) for go in (at_z, at_y, at_x) for o in (1, -1)]
    for dev in peers:
        pl.semaphore_signal(barrier, inc=1, device_id=dev, device_id_type=MESH)

    diag = lax.broadcasted_iota(jnp.int32, (BR, BR), 0) == lax.broadcasted_iota(jnp.int32, (BR, BR), 1)
    lane = lax.broadcasted_iota(jnp.int32, (BR, 128), 1)
    l_lse.wait()
    turned = [
        jnp.sum(jnp.where(diag, jnp.broadcast_to(lse_v[h : h + 1, :], (BR, BR)), 0.0), axis=1, keepdims=True)
        for h in range(2)
    ]
    qol[me, :, 512:] = jnp.where(lane == 0, turned[0], turned[1])

    for c in l_w:
        c.wait()

    @pl.loop(0, WD // 32)
    def _(i):
        rows = pl.ds(pl.multiple_of(i * 32, 32), 32)
        for n in range(2):
            hi, lo = split(w2f[n, rows, :])
            w2h[rows, n * WF : (n + 1) * WF] = hi
            w2l[rows, n * WF : (n + 1) * WF] = lo

    pl.semaphore_wait(barrier, len(peers))

    for c in l_rg:
        c.wait()
    zin, pr = {}, {}

    def zsend(s_from, s_to):
        o = 1 if s_to in (2, 4, 6) else -1
        zin[s_to] = send(rg.at[s_from, core], rg.at[s_to, core], at_z(o), "z", ("z", s_to))

    def psend(s):
        pr[s] = send(rg.at[s, core], rg.at[s, core], pair, "pair", ("pair", s))

    zsend(0, 1)
    zsend(0, 2)
    psend(0)
    for c in l_wd:
        c.wait()

    @pl.loop(0, WF // 128)
    def _(i):
        rows = pl.ds(pl.multiple_of(i * 128, 128), 128)
        hi, lo = split(wdf[rows, :])
        wdh[rows, :] = hi
        wdl[rows, :] = lo

    def rows_pass(*slots):
        for s in slots:
            zin[s].wait_recv()
            if s < 6:
                zsend(s, s + 2)
            psend(s)

    rows_pass(1, 2, 3)

    @pl.loop(0, WD // 64)
    def _(i):
        rows = pl.ds(pl.multiple_of(i * 64, 64), 64)
        hi, lo = split(wof[rows, :])
        woh[rows, :] = hi
        wol[rows, :] = lo

    def project(k):
        both = rg[4 * k : 4 * k + 4]
        resid = both[:, :, 0].reshape(128, WD)
        grad = both[:, :, 1].reshape(128, WD)
        squares = jnp.sum(resid * resid, axis=1, keepdims=True)
        part[k, :, :, :, 2688:] = jnp.broadcast_to(squares, (128, 128)).reshape(4, 4, 8, 128)
        xh, xl = split(resid * gain[...])
        xx = jnp.concatenate([xh, xl], axis=0)
        for n in range(7):
            cols = slice(n * 256, (n + 1) * 256)
            two = nn(xx, w2h[:, cols])
            part[k, :, :, :, cols] = (two[:128] + two[128:] + nn(xh, w2l[:, cols])).reshape(4, 4, 8, 256)
        gh, gl = split(grad)
        gg = jnp.concatenate([gh, gl], axis=0)
        for lo, hi in ((0, 256), (256, 512), (512, 768), (768, 896)):
            two = nt(gg, wdh[lo:hi, :])
            part[k, :, :, :, 1792 + lo : 1792 + hi] = (
                two[:128] + two[128:] + nt(gh, wdl[lo:hi, :])
            ).reshape(4, 4, 8, hi - lo)

    axes = ((at_x, x, at_y, y), (at_y, y, at_x, x))
    cs = (slice(0, HALF), slice(HALF, WIDTH))
    LO, HI = slice(0, 640), slice(640, HALF)

    def wrap(v, o):
        return lax.rem(v + (o + 4), 4)

    VIA = {2: 1, 1: -1, 0: 1, 3: -1}

    def at_piece(k, h, r, a):
        b = wrap(axes[h][3], r)
        return (k, b, a, slice(None), cs[h]) if h == 0 else (k, a, b, slice(None), cs[h])

    m1, m2 = {}, {}

    def rs1_send(k):
        for r in (2, 1, 0, 3):
            for h in range(2):
                go, av, _, _ = axes[h]
                m1[k, h, r] = send(
                    part.at[at_piece(k, h, r, wrap(av, 2))], r1.at[k, h, r], go(VIA[r]), "rs1r", ("r", k, h, r)
                )

    def rs1_direct(k):
        for r in (2, 1, 3, 0):
            for h in range(2):
                go, av, _, _ = axes[h]
                send(
                    part.at[at_piece(k, h, r, wrap(av, -VIA[r]))], c1.at[k, h, r, 1], go(-VIA[r]), "rs1d", ("c", k, h, r)
                )

    def rs1_relay(k):
        for r in (2, 1, 0, 3):
            for h in range(2):
                go, av, _, _ = axes[h]
                m1[k, h, r].wait_recv()
                r1[k, h, r] = r1[k, h, r] + part[at_piece(k, h, r, wrap(av, VIA[r]))]
                send(r1.at[k, h, r], c1.at[k, h, r, 0], go(VIA[r]), "rs1c", ("c", k, h, r))

    def rs1_final(k):
        for r in (2, 1, 3, 0):
            for h in range(2):
                _, av, go, _ = axes[h]
                arrived(("c", k, h, r), c1.at[k, h, r])
                q1[k, h, r] = part[at_piece(k, h, r, av)] + c1[k, h, r, 0] + c1[k, h, r, 1]
                if r == 2:
                    m2[k, h, 1] = send(
                        q1.at[k, h, 2, :, LO], r2.at[k, h, 0, :, LO], go(1), "rs2", ("rp", k, h)
                    )
                    m2[k, h, -1] = send(
                        q1.at[k, h, 2, :, HI], r2.at[k, h, 1, :, HI], go(-1), "rs2", ("rm", k, h)
                    )
                elif r == 1:
                    send(q1.at[k, h, 1, :, HI], c2.at[k, h, 0, :, HI], go(1), "rs2", ("c2", k, h))
                elif r == 3:
                    send(q1.at[k, h, 3, :, LO], c2.at[k, h, 1, :, LO], go(-1), "rs2", ("c2", k, h))

    def rs2_relay(k):
        for h in range(2):
            _, _, go, _ = axes[h]
            m2[k, h, 1].wait_recv()
            r2[k, h, 0, :, LO] = r2[k, h, 0, :, LO] + q1[k, h, 1, :, LO]
            send(r2.at[k, h, 0, :, LO], c2.at[k, h, 0, :, LO], go(1), "rs2", ("c2", k, h))
            m2[k, h, -1].wait_recv()
            r2[k, h, 1, :, HI] = r2[k, h, 1, :, HI] + q1[k, h, 3, :, HI]
            send(r2.at[k, h, 1, :, HI], c2.at[k, h, 1, :, HI], go(-1), "rs2", ("c2", k, h))

    def gate(k):
        sums = []
        for h in range(2):
            arrived(("c2", k, h), c2.at[k, h])
            sums.append(q1[k, h, 0] + c2[k, h, 0] + c2[k, h, 1])
        total = jnp.concatenate(sums, axis=1)
        inv = lax.rsqrt(total[:, 2688:] / D + EPS)
        inv1 = inv[:, 0:1]
        gate_raw, up_raw, d_hidden = total[:, 0:896], total[:, 896:1792], total[:, 1792:2688]
        gate_out, up_out = gate_raw * inv1, up_raw * inv1
        sig = jax.nn.sigmoid(gate_out)
        activated = gate_out * sig
        d_up = d_hidden * activated
        d_gate = d_hidden * up_out * sig * (1.0 + gate_out * (1.0 - sig))
        dot = jnp.sum(d_gate * gate_raw + d_up * up_raw, axis=1, keepdims=True)
        coef = inv * inv * inv * dot / D
        lane = lax.broadcasted_iota(jnp.int32, (8, 128), 1)
        full[k, y, x, :, 0:896] = activated * up_out
        full[k, y, x, :, 896:1792] = d_gate
        full[k, y, x, :, 1792:2688] = d_up
        full[k, y, x, :, 2688:] = jnp.where(lane < 64, inv, coef)

    def sub(c, part_of):
        return slice(c.start + part_of.start, c.start + part_of.stop)

    def fsend(k, h, r, a, dev, out, into, cols=None):
        at = at_piece(k, h, r, a)
        if cols is not None:
            at = at[:-1] + (sub(cs[h], cols),)
        return send(full.at[at], full.at[at], dev, out, into)

    g1, g2 = {}, {}

    def ag_across(k, h, r):
        go, av, _, _ = axes[h]
        for d in (1, -1):
            into = ("a", k, h, r) if d == VIA[r] else ("done", k)
            g2[k, h, r, d] = fsend(k, h, r, av, go(d), ("a", k), into)

    def ag_own(k):
        for h in range(2):
            _, av, go, _ = axes[h]
            for d in (1, -1):
                g1[k, h, d] = fsend(k, h, 0, av, go(d), "ag1", ("b", k, h, d))
        for h in range(2):
            ag_across(k, h, 0)

    def ag_near(k):
        for h in range(2):
            _, av, go, _ = axes[h]
            g1[k, h, 1].wait_recv()
            fsend(k, h, 3, av, go(1), "ag1", ("b2", k, h), LO)
            g1[k, h, -1].wait_recv()
            fsend(k, h, 1, av, go(-1), "ag1", ("b2", k, h), HI)
        for r in (3, 1):
            for h in range(2):
                ag_across(k, h, r)

    def ag_far(k):
        for h in range(2):
            arrived(("b2", k, h), q1.at[k, h, 0])
            ag_across(k, h, 2)

    def ag_pass(k, r):
        for h in range(2):
            go, av, _, _ = axes[h]
            g2[k, h, r, VIA[r]].wait_recv()
            fsend(k, h, r, wrap(av, -VIA[r]), go(VIA[r]), "pass", ("done", k))

    def ag_done(k):
        arrived(("done", k), full.at[k, :, :, :, cs[0]])

    pf = {}

    def input_grad(k):
        ag_done(k)
        dgu = full[k, :, :, :, 896:2688].reshape(128, 1792)
        tile = full[k, :, :, :, 2688:].reshape(128, 128)
        inv, coef = tile[:, 0:1], tile[:, 64:65]
        dn = three(dgu, w2h[...], w2l[...], nt)
        resid = rg[4 * k : 4 * k + 4, :, 0].reshape(128, WD)
        t = dn * gain[...] * inv - resid * coef
        tpart[k] = t.reshape(4, 2, BR, WD)
        pf[k] = send(tpart.at[k, :, other], tpair.at[k], pair, "pf", ("pf", k))

    def input_grad_send(k):
        pf[k].wait_recv()
        usum[k] = tpart[k, :, core] + tpair[k]
        for s in range(4 * k + 3, max(4 * k, 1) - 1, -1):
            send(usum.at[k, s % 4], rz.at[s], at_z(OFF[s]), "zf", "zf")

    def weight_grads():
        inv = full[:, :, :, :, 2688:].reshape(ROWS, 128)[:, 0:1]
        both = rg[...]
        resid = both[:, :, 0].reshape(ROWS, WD)
        grad = both[:, :, 1].reshape(ROWS, WD)
        nt_ = (resid * gain[...] * inv).T
        nh, nl = split(nt_)
        nn2 = jnp.concatenate([nh, nl], axis=0)
        for n in range(7):
            cols = slice(896 + n * 256, 896 + (n + 1) * 256)
            bh, bl = split(full[:, :, :, :, cols].reshape(ROWS, 256))
            two = nn(nn2, bh)
            gw2[:, n * 256 : (n + 1) * 256] = two[:WD] + two[WD:] + nn(nh, bl)
        gh, gl = split(grad)
        for n in range(7):
            cols = slice(n * 128, (n + 1) * 128)
            ht = full[:, :, :, :, cols].reshape(ROWS, 128).T
            hh, hl = split(ht)
            two = nn(jnp.concatenate([hh, hl], axis=0), gh)
            gwd[cols, :] = two[:128] + two[128:] + nn(hh, gl)

    def attention_split():
        for c in l_kv:
            c.wait()
        arrived("kv", kv.at[:, 0])

        @pl.loop(0, 16)
        def _(i):
            m, j = i // 8, lax.rem(i, 8)
            src = pl.ds(pl.multiple_of(j * 128, 128), 128)
            dst = pl.ds(pl.multiple_of(i * 128, 128), 128)
            for n, out in ((0, k3), (1, v3)):
                hi, lo = split(kv[n, m, src, :])
                out[dst, 0:128] = hi
                out[dst, 128:256] = lo
                out[dst, 256:384] = hi

    def attention_probs(h):
        q = qol[:, :, h * HD : (h + 1) * HD].reshape(ROWS, HD)
        lse = qol[:, :, 512:].reshape(ROWS, 128)[:, h : h + 1]
        qh, ql = split(q)
        q3 = jnp.concatenate([qh, qh, ql], axis=1)

        @pl.loop(0, 4)
        def _(i):
            keys = pl.ds(pl.multiple_of(i * 512, 512), 512)
            s = nt(q3, k3[keys, :]) * SCALE
            first = (i // 2) * (KEYS * NCTX) + me * KEYS + lax.rem(i, 2) * 512
            pos = first + lax.broadcasted_iota(jnp.int32, (ROWS, 512), 1)
            row = (CONTEXT - ROWS) + lax.broadcasted_iota(jnp.int32, (ROWS, 512), 0)
            probs[h, :, keys] = jnp.where(pos <= row, jnp.exp(s - lse), 0.0)

    def rows_pair(k):
        for s in range(4 * k, 4 * k + 4):
            pr[s].wait_recv()

    outs = []

    def start_kv():
        send(key_h.at[0], kv.at[0, core], pair, "kv", "kv")
        send(val_h.at[0], kv.at[1, core], pair, "kv", "kv")

    def start_qo():
        for c in l_qol:
            c.wait()
        for o in ctx_offsets:
            send(qol.at[me], qol.at[me], at_ctx(*o), "qo", "qo")

    gz = {}

    def resid_own():
        total = rg[0, core, 1] + usum[0, 0]
        arrived("zf", rz.at[1:8])
        for s in range(1, 8):
            total = total + rz[s]
        gres[wide] = total
        for s in range(7, 0, -1):
            gz[s] = send(gres.at[wide], gres.at[wide], at_z(OFF[s]), "g", ("g", s))
        send(gres.at[wide], gres.at[wide], pair, "g", "gp")
        outs.append(local(gres.at[wide], gres_o))

    def resid_all():
        for s in range(1, 8):
            gz[s].wait_recv()
            w = 2 * lax.rem(z + (NZ - OFF[s]), NZ) + core
            send(gres.at[w], gres.at[w], pair, "g", "gp")

    def resid_pair():
        arrived("gp", gres.at[0:8])

    def d_attn_part():
        gh, gl = split(gres[...].reshape(ROWS, WD))
        gg = jnp.concatenate([gh, gl], axis=0)
        for h in range(2):
            cols = slice(h * HD, (h + 1) * HD)
            two = nt(gg, woh[cols, :])
            da[h] = (two[:ROWS] + two[ROWS:] + nt(gh, wol[cols, :])).reshape(16, BR, HD)
            for n, o in enumerate(ctx_offsets):
                send(da.at[h, ctx_of(*o)], rda.at[h, n], at_ctx(*o), "di", ("di", h))

    def out_grad():
        oh, ol = split(qol[:, :, 256:512].reshape(ROWS, WD).T)
        eh, el = split(gres[...].reshape(ROWS, WD))
        two = nn(jnp.concatenate([oh, ol], axis=0), eh)
        gwo[...] = two[:WD] + two[WD:] + nn(oh, el)
        outs.append(local(gwo, gwo_o))

    def d_attn_sum(h):
        arrived(("di", h), rda.at[h])
        own = da[h, me]
        for n in range(NCTX - 1):
            own = own + rda[h, n]
        dat[h, me] = own
        for o in ctx_offsets:
            send(dat.at[h, me], dat.at[h, me], at_ctx(*o), "do", ("do", h))

    def d_attn_all(h):
        arrived(("do", h), rda.at[h])

    def query_grad(h):
        d_attn = dat[h].reshape(ROWS, HD)
        o = qol[:, :, 256 + h * HD : 256 + (h + 1) * HD].reshape(ROWS, HD)
        delta = jnp.sum(d_attn * o, axis=1, keepdims=True)
        dh, dl = split(d_attn)
        d3 = jnp.concatenate([dh, dh, dl], axis=1)
        acc[...] = jnp.zeros_like(acc)

        for i in range(4):
            keys = slice(i * 512, (i + 1) * 512)
            g = probs[h, :, keys] * (nt(d3, v3[keys, :]) - delta)
            gh, gl = split(g)
            acc[...] += nn(jnp.concatenate([gh, gl], axis=0), k3[keys, 0:256])

        a = acc[...]
        out = (a[:ROWS, :HD] + a[:ROWS, HD:] + a[ROWS:, :HD] + a[ROWS:, HD:]) * SCALE
        dq[h] = out.reshape(16, BR, HD)
        for n, o in enumerate(ctx_offsets):
            send(dq.at[h, ctx_of(*o)], rdq.at[h, n], at_ctx(*o), "qi", ("qi", h))

    def query_sum(h):
        arrived(("qi", h), rdq.at[h])
        own = dq[h, me]
        for n in range(NCTX - 1):
            own = own + rdq[h, n]
        gqs[:, h * HD : (h + 1) * HD] = own

    def store_weights():
        outs.append(local(gw2.at[:, 0:WF], gwg_o))
        outs.append(local(gw2.at[:, WF : 2 * WF], gwu_o))
        outs.append(local(gwd, gwd_o))

    def qo_wait():
        arrived("qo", qol.at[0:15])

    def finish():
        outs.append(local(gqs, gq_o))
        sixteen = full.at[0, :, :, :, cs[0]]
        for out, like in (
            ("z", rg.at[1:8, 0]), ("pair", rg.at[:, 0]), ("kv", kv.at[:, 0]), ("qo", qol.at[0:15]),
            ("rs1r", sixteen), ("rs1d", sixteen), ("rs1c", sixteen), ("rs2", q1.at[:, :, 0:3]),
            ("ag1", q1.at[:, :, 0:3]), (("a", 0), sixteen), (("a", 1), sixteen), ("pass", sixteen),
            ("pf", tpair), ("zf", rz.at[1:8]), ("g", gres.at[0:15]), ("di", rda), ("do", rda), ("qi", rdq),
        ):
            gone(out, like)
        for c in outs:
            c.wait()

    rows_pair(0)
    project(0)
    rs1_send(0)
    rs1_direct(0)
    rows_pass(4, 5, 6)
    rs1_relay(0)
    rows_pass(7)
    rows_pair(1)
    project(1)
    rs1_send(1)
    rs1_final(0)
    rs1_direct(1)
    start_kv()
    rs2_relay(0)
    rs1_relay(1)
    gate(0)
    ag_own(0)
    rs1_final(1)
    ag_near(0)
    ag_pass(0, 0)
    rs2_relay(1)
    ag_far(0)
    gate(1)
    ag_own(1)
    ag_pass(0, 3)
    ag_pass(0, 1)
    ag_near(1)
    ag_pass(0, 2)
    ag_pass(1, 0)
    ag_far(1)
    ag_pass(1, 3)
    ag_pass(1, 1)
    ag_pass(1, 2)
    input_grad(0)
    input_grad_send(0)
    input_grad(1)
    input_grad_send(1)
    start_qo()
    weight_grads()
    store_weights()
    attention_split()
    resid_own()
    resid_all()
    resid_pair()
    d_attn_part()
    qo_wait()
    out_grad()
    attention_probs(0)
    d_attn_sum(0)
    d_attn_sum(1)
    attention_probs(1)
    d_attn_all(0)
    query_grad(0)
    d_attn_all(1)
    query_grad(1)
    query_sum(0)
    query_sum(1)
    finish()


def put(*refs):
    sem = refs[12]
    copies = [pltpu.make_async_copy(refs[n], refs[6 + n], sem.at[n]) for n in range(6)]
    for c in copies:
        c.start()
    for c in copies:
        c.wait()


def shards(residual, grad_out, norm_gain, w_gate, w_up, w_down, w_out, queries, attn_out, log_sum_exp, key_cache, value_cache):
    operands = (
        residual, grad_out, norm_gain.reshape(1, WD), w_gate, w_up, w_down, w_out,
        queries, attn_out, log_sum_exp, key_cache, value_cache,
    )
    V = pltpu.VMEM
    shape = jax.ShapeDtypeStruct
    scratch = [
        V((8, 2, 2, BR, WD), F32),
        V((1, WD), F32), V((2, BR), F32),
        V((2, WD, WF), F32), V((WF, WD), F32), V((WD, WD), F32),
        V((WD, 2 * WF), BF16), V((WD, 2 * WF), BF16),
        V((WF, WD), BF16), V((WF, WD), BF16),
        V((WD, WD), BF16), V((WD, WD), BF16),
        V((16, BR, 640), F32),
        V((2, 2, KEYS, HD), F32),
        V((2 * KEYS, 384), BF16), V((2 * KEYS, 384), BF16),
        V((2, 4, 4, 8, WIDTH), F32),
        V((2, 2, 4, 8, HALF), F32), V((2, 2, 4, 2, 8, HALF), F32),
        V((2, 2, 4, 8, HALF), F32),
        V((2, 2, 2, 8, HALF), F32), V((2, 2, 2, 8, HALF), F32),
        V((2, 4, 4, 8, WIDTH), F32),
        V((2, 4, 2, BR, WD), F32), V((2, 4, BR, WD), F32), V((2, 4, BR, WD), F32),
        V((8, BR, WD), F32),
        V((16, BR, WD), F32), V((2, 16, BR, HD), F32), V((2, 15, BR, HD), F32), V((2, 16, BR, HD), F32),
        V((2, ROWS, 2 * KEYS), F32),
        V((2 * ROWS, 2 * HD), F32),
        V((2, 16, BR, HD), F32), V((2, 15, BR, HD), F32),
        V((WD, 2 * WF), F32), V((WF, WD), F32), V((WD, WD), F32), V((BR, WD), F32),
        pltpu.SemaphoreType.DMA((18,)),
        pltpu.SemaphoreType.DMA((18,)),
        pltpu.SemaphoreType.DMA((108,)),
    ]
    hbm = pl.BlockSpec(memory_space=pltpu.HBM)
    anyspec = pl.BlockSpec(memory_space=pl.ANY)
    sent = pl.pallas_call(
        kernel,
        out_shape=(
            shape((WD, WF), F32), shape((WD, WF), F32), shape((WF, WD), F32),
            shape((WD, WD), F32), shape((BR, WD), F32), shape((BR, WD), F32),
        ),
        in_specs=[hbm] * 12,
        out_specs=(anyspec,) * 6,
        scratch_shapes=scratch,
        compiler_params=pltpu.CompilerParams(
            collective_id=0, has_side_effects=True, vmem_limit_bytes=LIMIT
        ),
    )(*[pltpu.with_memory_space_constraint(a, pltpu.HBM) for a in operands])
    return pl.pallas_call(
        put,
        out_shape=tuple(shape(o.shape, F32) for o in sent),
        in_specs=[anyspec] * 6,
        out_specs=(hbm,) * 6,
        scratch_shapes=[pltpu.SemaphoreType.DMA((6,))],
        compiler_params=pltpu.CompilerParams(vmem_limit_bytes=1024 * 1024),
    )(*sent)


def solution(mesh):
    torus = Mesh(mesh.devices.reshape(NZ, 2, NY, NX), ("z", "core", "y", "x"))
    wide, ctx = ("z", "core"), ("y", "x")
    return jax.shard_map(
        shards,
        mesh=torus,
        in_specs=(
            P(wide, ctx), P(wide, ctx), P(ctx), P(ctx, wide), P(ctx, wide), P(wide, ctx), P(wide, ctx),
            P(ctx, wide), P(ctx, wide), P(wide, ctx), P(wide, ctx, None), P(wide, ctx, None),
        ),
        out_specs=(P(ctx, wide), P(ctx, wide), P(wide, ctx), P(wide, ctx), P(wide, ctx), P(ctx, wide)),
        check_vma=False,
    )
```

```python
import math

import jax
import jax.numpy as jnp
from jax import lax
from jax.experimental import pallas as pl
from jax.experimental.pallas import tpu as pltpu
from jax.sharding import Mesh
from jax.sharding import PartitionSpec as P

MESH = pl.DeviceIdType.MESH
F32 = jnp.float32
BF16 = jnp.bfloat16
EPS = 1e-05
NZ, NX, NY = 8, 4, 4
NCTX = NX * NY
OFF = (0, 1, -1, 2, -2, 3, -3, 4)
SLOT = {o: s for s, o in enumerate(OFF)}
D, FF, HD = 4096, 14336, 128
WD, WF = D // NCTX, FF // 16
ROWS, BR = 256, 16
HALF = 11 * 128
WIDTH = 2 * HALF
KEYS = 1024
NSEM = 122
LIMIT = 48 * 1024 * 1024
CONTEXT = 32768
SCALE = 1.0 / math.sqrt(HD)

ORDER = (
    ("S", 0, 0, 2), ("D", 0, 1, 2), ("S", 0, 1, 2), ("D", 0, 0, 2), ("S", 0, 0, 1), ("S", 0, 0, 0), ("D", 0, 0, 3),
    ("D", 0, 0, 1), ("S", 0, 0, 3), ("D", 0, 0, 0), ("S", 0, 1, 0), ("S", 0, 1, 1), ("D", 0, 1, 3), ("S", 0, 1, 3),
    ("D", 0, 1, 1), ("D", 0, 1, 0), ("Z", 4), ("Z", 5, 6), ("R", 0, 0, 2), ("R", 0, 1, 2), ("R", 0, 0, 0), ("R", 0, 0, 1),
    ("R", 0, 1, 1), ("R", 0, 1, 0), ("R", 0, 0, 3), ("R", 0, 1, 3), ("Z", 7), ("J", 1), ("S", 1, 0, 3), ("S", 1, 1, 3),
    ("S", 1, 1, 2), ("S", 1, 0, 2), ("F", 0, 0, 2), ("F", 0, 1, 2), ("S", 1, 1, 0), ("D", 1, 1, 2), ("S", 1, 0, 1),
    ("D", 1, 1, 3), ("S", 1, 1, 1), ("S", 1, 0, 0), ("D", 1, 0, 3), ("D", 1, 1, 0), ("D", 1, 0, 2), ("F", 0, 0, 1),
    ("F", 0, 1, 1), ("F", 0, 1, 3), ("F", 0, 0, 0), ("F", 0, 0, 3), ("R", 1, 1, 2), ("R", 1, 0, 2), ("R", 1, 0, 3),
    ("T", 0, 1, -1), ("T", 0, 0, -1), ("T", 0, 1, 1), ("T", 0, 0, 1), ("D", 1, 1, 1), ("D", 1, 0, 1), ("R", 1, 1, 3),
    ("R", 1, 0, 1), ("D", 1, 0, 0), ("R", 1, 0, 0), ("F", 0, 1, 0), ("R", 1, 1, 1), ("R", 1, 1, 0), ("F", 1, 1, 2),
    ("F", 1, 0, 2), ("G", 0), ("O", 0, 1, 1), ("O", 0, 1, -1), ("O", 0, 0, -1), ("O", 0, 0, 1), ("A", 0, 1, 0, -1),
    ("A", 0, 1, 0, 1), ("F", 1, 0, 1), ("A", 0, 0, 0, 1), ("A", 0, 0, 0, -1), ("F", 1, 1, 3), ("F", 1, 1, 1),
    ("F", 1, 0, 3), ("T", 1, 1, -1), ("T", 1, 0, -1), ("T", 1, 0, 1), ("T", 1, 1, 1), ("A", 0, 1, 3, 1),
    ("N", 0, 1, 1), ("N", 0, 0, -1), ("A", 0, 1, 3, -1), ("N", 0, 1, -1), ("A", 0, 0, 3, -1), ("A", 0, 1, 1, -1),
    ("A", 0, 0, 1, -1), ("F", 1, 1, 0), ("N", 0, 0, 1), ("A", 0, 1, 1, 1), ("A", 0, 0, 3, 1), ("F", 1, 0, 0),
    ("A", 0, 0, 1, 1), ("G", 1), ("O", 1, 0, -1), ("O", 1, 1, -1), ("O", 1, 1, 1), ("O", 1, 0, 1), ("P", 0, 0, 0),
    ("A", 0, 1, 2, 1), ("A", 0, 1, 2, -1), ("A", 1, 0, 0, -1), ("A", 0, 0, 2, 1), ("P", 0, 1, 0), ("A", 1, 0, 0, 1),
    ("A", 1, 1, 0, -1), ("A", 1, 1, 0, 1), ("A", 0, 0, 2, -1), ("N", 1, 0, -1), ("N", 1, 1, -1), ("A", 1, 0, 1, -1),
    ("A", 1, 1, 3, -1), ("N", 1, 0, 1), ("A", 1, 1, 1, -1), ("A", 1, 1, 3, 1), ("A", 1, 0, 3, -1), ("N", 1, 1, 1),
    ("A", 1, 0, 1, 1), ("P", 0, 0, 1), ("A", 1, 0, 3, 1), ("P", 0, 1, 2), ("P", 0, 0, 3), ("P", 0, 1, 1),
    ("A", 1, 0, 2, 1), ("A", 1, 1, 2, 1), ("P", 0, 1, 3), ("P", 1, 0, 0), ("A", 1, 1, 2, -1), ("A", 1, 1, 1, 1),
    ("P", 0, 0, 2), ("A", 1, 0, 2, -1), ("P", 1, 1, 0), ("P", 1, 1, 3), ("P", 1, 1, 1), ("P", 1, 0, 3), ("P", 1, 0, 1),
    ("P", 1, 0, 2), ("P", 1, 1, 2),
)


def split(v):
    hi = v.astype(BF16)
    return hi, (v - hi.astype(F32)).astype(BF16)


def nn(a, b):
    return lax.dot_general(a, b, (((1,), (0,)), ((), ())), preferred_element_type=F32)


def nt(a, b):
    return lax.dot_general(a, b, (((1,), (1,)), ((), ())), preferred_element_type=F32)


def three(a, bh, bl, dot):
    ah, al = split(a)
    m = a.shape[0]
    both = dot(jnp.concatenate([ah, al], axis=0), bh)
    return both[:m] + both[m:] + dot(ah, bl)


def kernel(
    resid_h, grad_h, gain_h, wg_h, wu_h, wd_h, wo_h, q_h, o_h, lse_h, key_h, val_h,
    gwg_o, gwu_o, gwd_o, gwo_o, gres_o, gq_o,
    rg, gain, lse_v, w2f, wdf, wof, w2h, w2l, wdh, wdl, woh, wol, qol, kv, k3, v3,
    part, r1, c1, q1, r2, c2, full, tpart, tpair, usum, rz, gres, da, rda, dat,
    probs, acc, dq, rdq, gw2, gwd, gwo, gqs,
    lsem, ssem, rsem,
):
    z, core = lax.axis_index("z"), lax.axis_index("core")
    y, x = lax.axis_index("y"), lax.axis_index("x")
    me = y * NX + x
    other = 1 - core
    wide = 2 * z + core

    counter = {"l": 0}
    out_at, in_at = {}, {}

    def local(src, dst):
        copy = pltpu.make_async_copy(src, dst, lsem.at[counter["l"]])
        counter["l"] += 1
        copy.start()
        return copy

    def transfer(src, dst, out, into, dev):
        return pltpu.make_async_remote_copy(
            src_ref=src, dst_ref=dst,
            send_sem=ssem.at[out_at.setdefault(out, len(out_at))],
            recv_sem=rsem.at[in_at.setdefault(into, len(in_at))],
            device_id=dev, device_id_type=MESH,
        )

    def send(src, dst, dev, out, into):
        copy = transfer(src, dst, out, into, dev)
        copy.start()
        return copy

    def arrived(into, like):
        transfer(like, like, next(iter(out_at)), into, pair).wait_recv()

    def gone(out, like):
        transfer(like, like, out, next(iter(in_at)), pair).wait_send()

    def at_z(o):
        return {"z": lax.rem(z + (o + NZ), NZ)}

    def at_x(o):
        return {"x": lax.rem(x + (o + NX), NX)}

    def at_y(o):
        return {"y": lax.rem(y + (o + NY), NY)}

    pair = {"core": other}
    ctx_offsets = sorted(
        [(dy, dx) for dy in range(NY) for dx in range(NX) if (dy, dx) != (0, 0)],
        key=lambda o: -(min(o[0], 4 - o[0]) + min(o[1], 4 - o[1])),
    )

    def at_ctx(dy, dx):
        return {"y": lax.rem(y + dy, NY), "x": lax.rem(x + dx, NX)}

    def ctx_of(dy, dx):
        return lax.rem(y + dy, NY) * NX + lax.rem(x + dx, NX)

    l_rg = [local(resid_h, rg.at[0, core, 0]), local(grad_h, rg.at[0, core, 1])]
    l_lse = local(lse_h, lse_v)
    l_w = [local(wg_h, w2f.at[0]), local(wu_h, w2f.at[1])]
    l_wd = [local(wd_h, wdf), local(wo_h, wof), local(gain_h, gain)]
    l_qol = [local(q_h, qol.at[me, :, 0:256]), local(o_h, qol.at[me, :, 256:512])]
    l_kv = [local(key_h.at[0], kv.at[0, core]), local(val_h.at[0], kv.at[1, core])]

    barrier = pltpu.get_barrier_semaphore()
    peers = [pair] + [go(o) for go in (at_z, at_y, at_x) for o in (1, -1)]
    peers += [at_z(o) | pair for o in (1, -1)]
    for dev in peers:
        pl.semaphore_signal(barrier, inc=1, device_id=dev, device_id_type=MESH)

    pl.semaphore_wait(barrier, len(peers))

    for c in l_rg:
        c.wait()
    zin = {}

    def zsend(s_from, s_to):
        dev = at_z(1 if s_to in (2, 4, 6) else -1)
        for n in range(2):
            zin[s_to, n] = send(rg.at[s_from, core, n], rg.at[s_to, core, n], dev, "z", ("z", s_to, n))
        send(rg.at[s_from, core], rg.at[s_to, core], dev | pair, "x", ("x", s_to))

    zsend(0, 1)
    zsend(0, 2)
    send(rg.at[0, core], rg.at[0, core], pair, "p", ("x", 0))

    diag = lax.broadcasted_iota(jnp.int32, (BR, BR), 0) == lax.broadcasted_iota(jnp.int32, (BR, BR), 1)
    lane = lax.broadcasted_iota(jnp.int32, (BR, 128), 1)
    l_lse.wait()
    turned = [
        jnp.sum(jnp.where(diag, jnp.broadcast_to(lse_v[h : h + 1, :], (BR, BR)), 0.0), axis=1, keepdims=True)
        for h in range(2)
    ]
    qol[me, :, 512:] = jnp.where(lane == 0, turned[0], turned[1])

    for c in l_w:
        c.wait()

    @pl.loop(0, WD // 32)
    def _(i):
        rows = pl.ds(pl.multiple_of(i * 32, 32), 32)
        for n in range(2):
            hi, lo = split(w2f[n, rows, :])
            w2h[rows, n * WF : (n + 1) * WF] = hi
            w2l[rows, n * WF : (n + 1) * WF] = lo

    def rows_pass(*slots):
        for s in slots:
            for n in range(2):
                zin[s, n].wait_recv()
            if s < 6:
                zsend(s, s + 2)

    rows_pass(1, 2)
    for c in l_wd:
        c.wait()

    @pl.loop(0, WF // 128)
    def _(i):
        rows = pl.ds(pl.multiple_of(i * 128, 128), 128)
        hi, lo = split(wdf[rows, :])
        wdh[rows, :] = hi
        wdl[rows, :] = lo

    rows_pass(3)

    def split_out():
        @pl.loop(0, WD // 64)
        def _(i):
            rows = pl.ds(pl.multiple_of(i * 64, 64), 64)
            hi, lo = split(wof[rows, :])
            woh[rows, :] = hi
            wol[rows, :] = lo

    def project(k):
        both = rg[4 * k : 4 * k + 4]
        resid = both[:, :, 0].reshape(128, WD)
        grad = both[:, :, 1].reshape(128, WD)
        squares = jnp.sum(resid * resid, axis=1, keepdims=True)
        part[k, :, :, :, 2688:] = jnp.broadcast_to(squares, (128, 128)).reshape(4, 4, 8, 128)
        xh, xl = split(resid * gain[...])
        xx = jnp.concatenate([xh, xl], axis=0)
        for n in range(7):
            cols = slice(n * 256, (n + 1) * 256)
            two = nn(xx, w2h[:, cols])
            part[k, :, :, :, cols] = (two[:128] + two[128:] + nn(xh, w2l[:, cols])).reshape(4, 4, 8, 256)
        gh, gl = split(grad)
        gg = jnp.concatenate([gh, gl], axis=0)
        for lo, hi in ((0, 256), (256, 512), (512, 768), (768, 896)):
            two = nt(gg, wdh[lo:hi, :])
            part[k, :, :, :, 1792 + lo : 1792 + hi] = (
                two[:128] + two[128:] + nt(gh, wdl[lo:hi, :])
            ).reshape(4, 4, 8, hi - lo)

    axes = ((at_x, x, at_y, y), (at_y, y, at_x, x))
    cs = (slice(0, HALF), slice(HALF, WIDTH))
    LO, HI = slice(0, 640), slice(640, HALF)

    def wrap(v, o):
        return lax.rem(v + (o + 4), 4)

    VIA = {2: 1, 1: -1, 0: 1, 3: -1}

    def at_piece(k, h, r, a):
        b = wrap(axes[h][3], r)
        return (k, b, a, slice(None), cs[h]) if h == 0 else (k, a, b, slice(None), cs[h])

    m1, m2 = {}, {}

    seen = set()

    def once(key, wait):
        if key not in seen:
            seen.add(key)
            wait()

    def relay_send(k, h, r):
        go, av, _, _ = axes[h]
        m1[k, h, r] = send(
            part.at[at_piece(k, h, r, wrap(av, 2))], r1.at[k, h, r], go(VIA[r]), "rs1r", ("r", k, h, r)
        )

    def direct_send(k, h, r):
        go, av, _, _ = axes[h]
        send(part.at[at_piece(k, h, r, wrap(av, -VIA[r]))], c1.at[k, h, r, 1], go(-VIA[r]), "rs1d", ("c", k, h, r))

    def relay_add(k, h, r):
        go, av, _, _ = axes[h]
        m1[k, h, r].wait_recv()
        r1[k, h, r] = r1[k, h, r] + part[at_piece(k, h, r, wrap(av, VIA[r]))]
        send(r1.at[k, h, r], c1.at[k, h, r, 0], go(VIA[r]), "rs1c", ("c", k, h, r))

    def first_sum(k, h, r):
        _, av, go, _ = axes[h]
        arrived(("c", k, h, r), c1.at[k, h, r])
        q1[k, h, r] = part[at_piece(k, h, r, av)] + c1[k, h, r, 0] + c1[k, h, r, 1]
        if r == 2:
            for d, cols in ((1, LO), (-1, HI)):
                n = (1 - d) // 2
                m2[k, h, d] = send(
                    q1.at[k, h, 2, :, cols], r2.at[k, h, n, :, cols], go(d), "rs2", ("r2", k, h, d)
                )
        elif r == 1:
            send(q1.at[k, h, 1, :, HI], c2.at[k, h, 0, :, HI], go(1), "rs2", ("c2", k, h))
        elif r == 3:
            send(q1.at[k, h, 3, :, LO], c2.at[k, h, 1, :, LO], go(-1), "rs2", ("c2", k, h))

    def second_add(k, h, d):
        _, _, go, _ = axes[h]
        n, r, cols = (0, 1, LO) if d == 1 else (1, 3, HI)
        m2[k, h, d].wait_recv()
        r2[k, h, n, :, cols] = r2[k, h, n, :, cols] + q1[k, h, r, :, cols]
        send(r2.at[k, h, n, :, cols], c2.at[k, h, n, :, cols], go(d), "rs2", ("c2", k, h))

    def gate(k):
        sums = []
        for h in range(2):
            arrived(("c2", k, h), c2.at[k, h])
            sums.append(q1[k, h, 0] + c2[k, h, 0] + c2[k, h, 1])
        total = jnp.concatenate(sums, axis=1)
        inv = lax.rsqrt(total[:, 2688:] / D + EPS)
        inv1 = inv[:, 0:1]
        gate_raw, up_raw, d_hidden = total[:, 0:896], total[:, 896:1792], total[:, 1792:2688]
        gate_out, up_out = gate_raw * inv1, up_raw * inv1
        sig = jax.nn.sigmoid(gate_out)
        activated = gate_out * sig
        d_up = d_hidden * activated
        d_gate = d_hidden * up_out * sig * (1.0 + gate_out * (1.0 - sig))
        dot = jnp.sum(d_gate * gate_raw + d_up * up_raw, axis=1, keepdims=True)
        coef = inv * inv * inv * dot / D
        lane = lax.broadcasted_iota(jnp.int32, (8, 128), 1)
        full[k, y, x, :, 0:896] = activated * up_out
        full[k, y, x, :, 896:1792] = d_gate
        full[k, y, x, :, 1792:2688] = d_up
        full[k, y, x, :, 2688:] = jnp.where(lane < 64, inv, coef)

    def sub(c, part_of):
        return slice(c.start + part_of.start, c.start + part_of.stop)

    def fsend(k, h, r, a, dev, out, into, cols=None):
        at = at_piece(k, h, r, a)
        if cols is not None:
            at = at[:-1] + (sub(cs[h], cols),)
        return send(full.at[at], full.at[at], dev, out, into)

    g1, g2 = {}, {}

    def near(k, h, d):
        once(("b", k, h, d), g1[k, h, d].wait_recv)

    def across(k, h, r, d):
        go, av, _, _ = axes[h]
        if r == 3:
            near(k, h, 1)
        elif r == 1:
            near(k, h, -1)
        elif r == 2:
            once(("b2", k, h), lambda: arrived(("b2", k, h), q1.at[k, h, 0]))
        into = ("a", k, h, r) if d == VIA[r] else ("done", k)
        g2[k, h, r, d] = fsend(k, h, r, av, go(d), ("a", k), into)

    def own_send(k, h, d):
        _, av, go, _ = axes[h]
        g1[k, h, d] = fsend(k, h, 0, av, go(d), "ag1", ("b", k, h, d))

    def near_pass(k, h, d):
        _, av, go, _ = axes[h]
        near(k, h, d)
        fsend(k, h, 3 if d == 1 else 1, av, go(d), "ag1", ("b2", k, h), LO if d == 1 else HI)

    def across_pass(k, h, r):
        go, av, _, _ = axes[h]
        g2[k, h, r, VIA[r]].wait_recv()
        fsend(k, h, r, wrap(av, -VIA[r]), go(VIA[r]), "pass", ("done", k))

    def ag_done(k):
        arrived(("done", k), full.at[k, :, :, :, cs[0]])

    pf = {}

    def input_grad(k):
        ag_done(k)
        dgu = full[k, :, :, :, 896:2688].reshape(128, 1792)
        tile = full[k, :, :, :, 2688:].reshape(128, 128)
        inv, coef = tile[:, 0:1], tile[:, 64:65]
        dn = three(dgu, w2h[...], w2l[...], nt)
        resid = rg[4 * k : 4 * k + 4, :, 0].reshape(128, WD)
        t = dn * gain[...] * inv - resid * coef
        tpart[k] = t.reshape(4, 2, BR, WD)
        for n in (3, 2, 1, 0):
            pf[k, n] = send(tpart.at[k, n, other], tpair.at[k, n], pair, "pf", ("pf", k, n))

    def input_grad_send(k):
        for n in (3, 2, 1, 0):
            pf[k, n].wait_recv()
            usum[k, n] = tpart[k, n, core] + tpair[k, n]
            s = 4 * k + n
            if s:
                send(usum.at[k, n], rz.at[s], at_z(OFF[s]), "zf", "zf")

    def weight_grads():
        inv = full[:, :, :, :, 2688:].reshape(ROWS, 128)[:, 0:1]
        both = rg[...]
        resid = both[:, :, 0].reshape(ROWS, WD)
        grad = both[:, :, 1].reshape(ROWS, WD)
        nt_ = (resid * gain[...] * inv).T
        nh, nl = split(nt_)
        nn2 = jnp.concatenate([nh, nl], axis=0)
        for n in range(7):
            cols = slice(896 + n * 256, 896 + (n + 1) * 256)
            bh, bl = split(full[:, :, :, :, cols].reshape(ROWS, 256))
            two = nn(nn2, bh)
            gw2[:, n * 256 : (n + 1) * 256] = two[:WD] + two[WD:] + nn(nh, bl)
        gh, gl = split(grad)
        for n in range(7):
            cols = slice(n * 128, (n + 1) * 128)
            ht = full[:, :, :, :, cols].reshape(ROWS, 128).T
            hh, hl = split(ht)
            two = nn(jnp.concatenate([hh, hl], axis=0), gh)
            gwd[cols, :] = two[:128] + two[128:] + nn(hh, gl)

    def attention_split():
        for c in l_kv:
            c.wait()
        arrived("kv", kv.at[:, 0])

        @pl.loop(0, 16)
        def _(i):
            m, j = i // 8, lax.rem(i, 8)
            src = pl.ds(pl.multiple_of(j * 128, 128), 128)
            dst = pl.ds(pl.multiple_of(i * 128, 128), 128)
            for n, out in ((0, k3), (1, v3)):
                hi, lo = split(kv[n, m, src, :])
                out[dst, 0:128] = hi
                out[dst, 128:256] = lo
                out[dst, 256:384] = hi

    def attention_probs(h):
        q = qol[:, :, h * HD : (h + 1) * HD].reshape(ROWS, HD)
        lse = qol[:, :, 512:].reshape(ROWS, 128)[:, h : h + 1]
        qh, ql = split(q)
        q3 = jnp.concatenate([qh, qh, ql], axis=1)

        @pl.loop(0, 4)
        def _(i):
            keys = pl.ds(pl.multiple_of(i * 512, 512), 512)
            s = nt(q3, k3[keys, :]) * SCALE
            first = (i // 2) * (KEYS * NCTX) + me * KEYS + lax.rem(i, 2) * 512
            pos = first + lax.broadcasted_iota(jnp.int32, (ROWS, 512), 1)
            row = (CONTEXT - ROWS) + lax.broadcasted_iota(jnp.int32, (ROWS, 512), 0)
            probs[h, :, keys] = jnp.where(pos <= row, jnp.exp(s - lse), 0.0)

    def rows_pair(k):
        for s in range(4 * k, 4 * k + 4):
            arrived(("x", s), rg.at[s, 0])

    outs = []

    def start_kv():
        send(key_h.at[0], kv.at[0, core], pair, "kv", "kv")
        send(val_h.at[0], kv.at[1, core], pair, "kv", "kv")

    def start_qo():
        for c in l_qol:
            c.wait()
        for o in ctx_offsets:
            send(qol.at[me], qol.at[me], at_ctx(*o), "qo", "qo")

    gz = {}

    def resid_own():
        total = rg[0, core, 1] + usum[0, 0]
        arrived("zf", rz.at[1:8])
        for s in range(1, 8):
            total = total + rz[s]
        gres[wide] = total
        for s in range(7, 0, -1):
            gz[s] = send(gres.at[wide], gres.at[wide], at_z(OFF[s]), "g", ("g", s))
        send(gres.at[wide], gres.at[wide], pair, "g", ("gp", 0))
        outs.append(local(gres.at[wide], gres_o))

    def resid_from(s):
        return lax.rem(z + (NZ - OFF[s]), NZ)

    def resid_pass(g):
        for s in range(max(4 * g, 1), 4 * g + 4):
            gz[s].wait_recv()
            w = 2 * resid_from(s) + core
            send(gres.at[w], gres.at[w], pair, "g", ("gp", g))
        arrived(("gp", g), gres.at[0:4])

    def d_attn_part(g):
        blocks = [2 * resid_from(s) + p for s in range(4 * g, 4 * g + 4) for p in range(2)]
        gh, gl = split(jnp.concatenate([gres[w] for w in blocks], axis=0))
        gg = jnp.concatenate([gh, gl], axis=0)
        for h in range(2):
            cols = slice(h * HD, (h + 1) * HD)
            two = nt(gg, woh[cols, :])
            out = two[:128] + two[128:] + nt(gh, wol[cols, :])
            for n, w in enumerate(blocks):
                da[h, w] = out[n * BR : (n + 1) * BR]
            for w in blocks:

                @pl.when(w != me)
                def _(w=w):
                    dev = {"y": w // NX, "x": lax.rem(w, NX)}
                    send(da.at[h, w], rda.at[h, me], dev, "di", ("di", h))

    def out_grad():
        oh, ol = split(qol[:, :, 256:512].reshape(ROWS, WD).T)
        eh, el = split(gres[...].reshape(ROWS, WD))
        two = nn(jnp.concatenate([oh, ol], axis=0), eh)
        gwo[...] = two[:WD] + two[WD:] + nn(oh, el)
        outs.append(local(gwo, gwo_o))

    def d_attn_sum(h):
        arrived(("di", h), rda.at[h, 0:15])
        own = da[h, me]
        for o in ctx_offsets:
            own = own + rda[h, ctx_of(*o)]
        dat[h, me] = own
        for o in ctx_offsets:
            send(dat.at[h, me], dat.at[h, me], at_ctx(*o), "do", ("do", h))

    def d_attn_all(h):
        arrived(("do", h), rda.at[h, 0:15])

    def query_grad(h):
        d_attn = dat[h].reshape(ROWS, HD)
        o = qol[:, :, 256 + h * HD : 256 + (h + 1) * HD].reshape(ROWS, HD)
        delta = jnp.sum(d_attn * o, axis=1, keepdims=True)
        dh, dl = split(d_attn)
        d3 = jnp.concatenate([dh, dh, dl], axis=1)
        acc[...] = jnp.zeros_like(acc)

        for i in range(4):
            keys = slice(i * 512, (i + 1) * 512)
            g = probs[h, :, keys] * (nt(d3, v3[keys, :]) - delta)
            gh, gl = split(g)
            acc[...] += nn(jnp.concatenate([gh, gl], axis=0), k3[keys, 0:256])

        a = acc[...]
        out = (a[:ROWS, :HD] + a[:ROWS, HD:] + a[ROWS:, :HD] + a[ROWS:, HD:]) * SCALE
        dq[h] = out.reshape(16, BR, HD)
        for n, o in enumerate(ctx_offsets):
            send(dq.at[h, ctx_of(*o)], rdq.at[h, n], at_ctx(*o), "qi", ("qi", h))

    def query_sum(h):
        arrived(("qi", h), rdq.at[h])
        own = dq[h, me]
        for n in range(NCTX - 1):
            own = own + rdq[h, n]
        gqs[:, h * HD : (h + 1) * HD] = own

    def store_weights():
        outs.append(local(gw2.at[:, 0:WF], gwg_o))
        outs.append(local(gw2.at[:, WF : 2 * WF], gwu_o))
        outs.append(local(gwd, gwd_o))

    def qo_wait():
        arrived("qo", qol.at[0:15])

    def finish():
        outs.append(local(gqs, gq_o))
        sixteen = full.at[0, :, :, :, cs[0]]
        for out, like in (
            ("z", rg.at[1:8, 0]), ("x", rg.at[1:8, 0]), ("p", rg.at[0, 0]), ("kv", kv.at[:, 0]), ("qo", qol.at[0:15]),
            ("rs1r", sixteen), ("rs1d", sixteen), ("rs1c", sixteen), ("rs2", q1.at[:, :, 0:3]),
            ("ag1", q1.at[:, :, 0:3]), (("a", 0), sixteen), (("a", 1), sixteen), ("pass", sixteen),
            ("pf", tpair), ("zf", rz.at[1:8]), ("g", gres.at[0:15]), ("di", rda.at[:, 0:15]), ("do", rda.at[:, 0:15]), ("qi", rdq),
        ):
            gone(out, like)
        for c in outs:
            c.wait()

    def enter(k):
        rows_pair(k)
        project(k)
        if k == 1:
            start_kv()

    steps = {
        "S": relay_send, "D": direct_send, "R": relay_add, "F": first_sum, "T": second_add, "G": gate,
        "O": own_send, "A": across, "N": near_pass, "P": across_pass, "Z": rows_pass, "J": enter,
    }
    enter(0)
    for step in ORDER:
        steps[step[0]](*step[1:])
    input_grad(0)
    input_grad_send(0)
    input_grad(1)
    input_grad_send(1)
    start_qo()
    weight_grads()
    store_weights()
    attention_split()
    split_out()
    resid_own()
    resid_pass(0)
    d_attn_part(0)
    resid_pass(1)
    d_attn_part(1)
    qo_wait()
    out_grad()
    attention_probs(0)
    d_attn_sum(0)
    d_attn_sum(1)
    attention_probs(1)
    d_attn_all(0)
    query_grad(0)
    d_attn_all(1)
    query_grad(1)
    query_sum(0)
    query_sum(1)
    finish()


def put(*refs):
    sem = refs[12]
    copies = [pltpu.make_async_copy(refs[n], refs[6 + n], sem.at[n]) for n in range(6)]
    for c in copies:
        c.start()
    for c in copies:
        c.wait()


def shards(residual, grad_out, norm_gain, w_gate, w_up, w_down, w_out, queries, attn_out, log_sum_exp, key_cache, value_cache):
    operands = (
        residual, grad_out, norm_gain.reshape(1, WD), w_gate, w_up, w_down, w_out,
        queries, attn_out, log_sum_exp, key_cache, value_cache,
    )
    V = pltpu.VMEM
    shape = jax.ShapeDtypeStruct
    scratch = [
        V((8, 2, 2, BR, WD), F32),
        V((1, WD), F32), V((2, BR), F32),
        V((2, WD, WF), F32), V((WF, WD), F32), V((WD, WD), F32),
        V((WD, 2 * WF), BF16), V((WD, 2 * WF), BF16),
        V((WF, WD), BF16), V((WF, WD), BF16),
        V((WD, WD), BF16), V((WD, WD), BF16),
        V((16, BR, 640), F32),
        V((2, 2, KEYS, HD), F32),
        V((2 * KEYS, 384), BF16), V((2 * KEYS, 384), BF16),
        V((2, 4, 4, 8, WIDTH), F32),
        V((2, 2, 4, 8, HALF), F32), V((2, 2, 4, 2, 8, HALF), F32),
        V((2, 2, 4, 8, HALF), F32),
        V((2, 2, 2, 8, HALF), F32), V((2, 2, 2, 8, HALF), F32),
        V((2, 4, 4, 8, WIDTH), F32),
        V((2, 4, 2, BR, WD), F32), V((2, 4, BR, WD), F32), V((2, 4, BR, WD), F32),
        V((8, BR, WD), F32),
        V((16, BR, WD), F32), V((2, 16, BR, HD), F32), V((2, 16, BR, HD), F32), V((2, 16, BR, HD), F32),
        V((2, ROWS, 2 * KEYS), F32),
        V((2 * ROWS, 2 * HD), F32),
        V((2, 16, BR, HD), F32), V((2, 15, BR, HD), F32),
        V((WD, 2 * WF), F32), V((WF, WD), F32), V((WD, WD), F32), V((BR, WD), F32),
        pltpu.SemaphoreType.DMA((18,)),
        pltpu.SemaphoreType.DMA((19,)),
        pltpu.SemaphoreType.DMA((NSEM,)),
    ]
    hbm = pl.BlockSpec(memory_space=pltpu.HBM)
    anyspec = pl.BlockSpec(memory_space=pl.ANY)
    sent = pl.pallas_call(
        kernel,
        out_shape=(
            shape((WD, WF), F32), shape((WD, WF), F32), shape((WF, WD), F32),
            shape((WD, WD), F32), shape((BR, WD), F32), shape((BR, WD), F32),
        ),
        in_specs=[hbm] * 12,
        out_specs=(anyspec,) * 6,
        scratch_shapes=scratch,
        compiler_params=pltpu.CompilerParams(
            collective_id=0, has_side_effects=True, vmem_limit_bytes=LIMIT
        ),
    )(*[pltpu.with_memory_space_constraint(a, pltpu.HBM) for a in operands])
    return pl.pallas_call(
        put,
        out_shape=tuple(shape(o.shape, F32) for o in sent),
        in_specs=[anyspec] * 6,
        out_specs=(hbm,) * 6,
        scratch_shapes=[pltpu.SemaphoreType.DMA((6,))],
        compiler_params=pltpu.CompilerParams(vmem_limit_bytes=1024 * 1024),
    )(*sent)


def solution(mesh):
    torus = Mesh(mesh.devices.reshape(NZ, 2, NY, NX), ("z", "core", "y", "x"))
    wide, ctx = ("z", "core"), ("y", "x")
    return jax.shard_map(
        shards,
        mesh=torus,
        in_specs=(
            P(wide, ctx), P(wide, ctx), P(ctx), P(ctx, wide), P(ctx, wide), P(wide, ctx), P(wide, ctx),
            P(ctx, wide), P(ctx, wide), P(wide, ctx), P(wide, ctx, None), P(wide, ctx, None),
        ),
        out_specs=(P(ctx, wide), P(ctx, wide), P(wide, ctx), P(wide, ctx), P(wide, ctx), P(ctx, wide)),
        check_vma=False,
    )
```

```python
import math

import jax
import jax.numpy as jnp
from jax import lax
from jax.experimental import pallas as pl
from jax.experimental.pallas import tpu as pltpu
from jax.sharding import Mesh
from jax.sharding import PartitionSpec as P

MESH = pl.DeviceIdType.MESH
F32 = jnp.float32
BF16 = jnp.bfloat16
EPS = 1e-05
NZ, NX, NY = 8, 4, 4
NCTX = NX * NY
OFF = (0, 1, -1, 2, -2, 3, -3, 4)
SLOT = {o: s for s, o in enumerate(OFF)}
D, FF, HD = 4096, 14336, 128
WD, WF = D // NCTX, FF // 16
ROWS, BR = 256, 16
HALF = 11 * 128
WIDTH = 2 * HALF
KEYS = 1024
NSEM = 109
LIMIT = 48 * 1024 * 1024
CONTEXT = 32768
SCALE = 1.0 / math.sqrt(HD)

ORDER = (
    ("S", 0, 0, 2), ("D", 0, 1, 2), ("S", 0, 1, 2), ("D", 0, 0, 2), ("S", 0, 0, 1), ("S", 0, 0, 0), ("D", 0, 0, 3),
    ("D", 0, 0, 1), ("S", 0, 0, 3), ("D", 0, 0, 0), ("S", 0, 1, 0), ("S", 0, 1, 1), ("D", 0, 1, 3), ("S", 0, 1, 3),
    ("D", 0, 1, 1), ("D", 0, 1, 0), ("Z", 4), ("Z", 5, 6), ("R", 0, 0, 2), ("R", 0, 1, 2), ("R", 0, 0, 0), ("R", 0, 0, 1),
    ("R", 0, 1, 1), ("R", 0, 1, 0), ("R", 0, 0, 3), ("R", 0, 1, 3), ("Z", 7), ("J", 1), ("S", 1, 0, 3), ("S", 1, 1, 3),
    ("S", 1, 1, 2), ("S", 1, 0, 2), ("F", 0, 0, 2), ("F", 0, 1, 2), ("S", 1, 1, 0), ("D", 1, 1, 2), ("S", 1, 0, 1),
    ("D", 1, 1, 3), ("S", 1, 1, 1), ("S", 1, 0, 0), ("D", 1, 0, 3), ("D", 1, 1, 0), ("D", 1, 0, 2), ("F", 0, 0, 1),
    ("F", 0, 1, 1), ("F", 0, 1, 3), ("F", 0, 0, 0), ("F", 0, 0, 3), ("R", 1, 1, 2), ("R", 1, 0, 2), ("R", 1, 0, 3),
    ("T", 0, 1, -1), ("T", 0, 0, -1), ("T", 0, 1, 1), ("T", 0, 0, 1), ("D", 1, 1, 1), ("D", 1, 0, 1), ("R", 1, 1, 3),
    ("R", 1, 0, 1), ("D", 1, 0, 0), ("R", 1, 0, 0), ("F", 0, 1, 0), ("R", 1, 1, 1), ("R", 1, 1, 0), ("F", 1, 1, 2),
    ("F", 1, 0, 2), ("G", 0), ("O", 0, 1, 1), ("O", 0, 1, -1), ("O", 0, 0, -1), ("O", 0, 0, 1), ("A", 0, 1, 0, -1),
    ("A", 0, 1, 0, 1), ("F", 1, 0, 1), ("A", 0, 0, 0, 1), ("A", 0, 0, 0, -1), ("F", 1, 1, 3), ("F", 1, 1, 1),
    ("F", 1, 0, 3), ("T", 1, 1, -1), ("T", 1, 0, -1), ("T", 1, 0, 1), ("T", 1, 1, 1), ("A", 0, 1, 3, 1),
    ("N", 0, 1, 1), ("N", 0, 0, -1), ("A", 0, 1, 3, -1), ("N", 0, 1, -1), ("A", 0, 0, 3, -1), ("A", 0, 1, 1, -1),
    ("A", 0, 0, 1, -1), ("F", 1, 1, 0), ("N", 0, 0, 1), ("A", 0, 1, 1, 1), ("A", 0, 0, 3, 1), ("F", 1, 0, 0),
    ("A", 0, 0, 1, 1), ("G", 1), ("O", 1, 0, -1), ("O", 1, 1, -1), ("O", 1, 1, 1), ("O", 1, 0, 1), ("P", 0, 0, 0),
    ("A", 0, 1, 2, 1), ("A", 0, 1, 2, -1), ("A", 1, 0, 0, -1), ("A", 0, 0, 2, 1), ("P", 0, 1, 0), ("A", 1, 0, 0, 1),
    ("A", 1, 1, 0, -1), ("A", 1, 1, 0, 1), ("A", 0, 0, 2, -1), ("N", 1, 0, -1), ("N", 1, 1, -1), ("A", 1, 0, 1, -1),
    ("A", 1, 1, 3, -1), ("N", 1, 0, 1), ("A", 1, 1, 1, -1), ("A", 1, 1, 3, 1), ("A", 1, 0, 3, -1), ("N", 1, 1, 1),
    ("A", 1, 0, 1, 1), ("P", 0, 0, 1), ("A", 1, 0, 3, 1), ("P", 0, 1, 2), ("P", 0, 0, 3), ("P", 0, 1, 1),
    ("A", 1, 0, 2, 1), ("A", 1, 1, 2, 1), ("P", 0, 1, 3), ("P", 1, 0, 0), ("A", 1, 1, 2, -1), ("A", 1, 1, 1, 1),
    ("P", 0, 0, 2), ("A", 1, 0, 2, -1), ("P", 1, 1, 0), ("P", 1, 1, 3), ("P", 1, 1, 1), ("P", 1, 0, 3), ("P", 1, 0, 1),
    ("P", 1, 0, 2), ("P", 1, 1, 2),
)


def split(v):
    hi = v.astype(BF16)
    return hi, (v - hi.astype(F32)).astype(BF16)


def nn(a, b):
    return lax.dot_general(a, b, (((1,), (0,)), ((), ())), preferred_element_type=F32)


def nt(a, b):
    return lax.dot_general(a, b, (((1,), (1,)), ((), ())), preferred_element_type=F32)


def three(a, bh, bl, dot):
    ah, al = split(a)
    m = a.shape[0]
    both = dot(jnp.concatenate([ah, al], axis=0), bh)
    return both[:m] + both[m:] + dot(ah, bl)


def kernel(
    resid_h, grad_h, gain_h, wg_h, wu_h, wd_h, wo_h, q_h, o_h, lse_h, key_h, val_h,
    gwg_o, gwu_o, gwd_o, gwo_o, gres_o, gq_o,
    rg, gain, lse_v, w2f, wdf, wof, w2h, w2l, wdh, wdl, woh, wol, qol, kv, k3, v3,
    part, r1, c1, q1, r2, c2, full, tpart, tpair, usum, rz, gres, da, rda, dat,
    probs, acc, dq, rdq, gw2, gwd, gwo, gqs,
    lsem, ssem, rsem,
):
    z, core = lax.axis_index("z"), lax.axis_index("core")
    y, x = lax.axis_index("y"), lax.axis_index("x")
    me = y * NX + x
    other = 1 - core
    wide = 2 * z + core

    counter = {"l": 0}
    out_at, in_at = {}, {}

    def local(src, dst):
        copy = pltpu.make_async_copy(src, dst, lsem.at[counter["l"]])
        counter["l"] += 1
        copy.start()
        return copy

    def transfer(src, dst, out, into, dev):
        return pltpu.make_async_remote_copy(
            src_ref=src, dst_ref=dst,
            send_sem=ssem.at[out_at.setdefault(out, len(out_at))],
            recv_sem=rsem.at[in_at.setdefault(into, len(in_at))],
            device_id=dev, device_id_type=MESH,
        )

    def send(src, dst, dev, out, into):
        copy = transfer(src, dst, out, into, dev)
        copy.start()
        return copy

    def arrived(into, like):
        transfer(like, like, next(iter(out_at)), into, pair).wait_recv()

    def gone(out, like):
        transfer(like, like, out, next(iter(in_at)), pair).wait_send()

    def at_z(o):
        return {"z": lax.rem(z + (o + NZ), NZ)}

    def at_x(o):
        return {"x": lax.rem(x + (o + NX), NX)}

    def at_y(o):
        return {"y": lax.rem(y + (o + NY), NY)}

    pair = {"core": other}
    ctx_offsets = sorted(
        [(dy, dx) for dy in range(NY) for dx in range(NX) if (dy, dx) != (0, 0)],
        key=lambda o: -(min(o[0], 4 - o[0]) + min(o[1], 4 - o[1])),
    )

    def at_ctx(dy, dx):
        return {"y": lax.rem(y + dy, NY), "x": lax.rem(x + dx, NX)}

    def ctx_of(dy, dx):
        return lax.rem(y + dy, NY) * NX + lax.rem(x + dx, NX)

    l_rg = [local(resid_h, rg.at[0, core, 0]), local(grad_h, rg.at[0, core, 1])]
    l_lse = local(lse_h, lse_v)
    l_w = [local(wg_h, w2f.at[0]), local(wu_h, w2f.at[1])]
    l_wd = [local(wd_h, wdf), local(wo_h, wof), local(gain_h, gain)]
    l_qol = [local(q_h, qol.at[me, :, 0:256]), local(o_h, qol.at[me, :, 256:512])]
    l_kv = [local(key_h.at[0], kv.at[0, core]), local(val_h.at[0], kv.at[1, core])]

    barrier = pltpu.get_barrier_semaphore()
    peers = [pair] + [go(o) for go in (at_z, at_y, at_x) for o in (1, -1)]
    peers += [at_z(o) | pair for o in (1, -1)]
    for dev in peers:
        pl.semaphore_signal(barrier, inc=1, device_id=dev, device_id_type=MESH)

    pl.semaphore_wait(barrier, len(peers))

    for c in l_rg:
        c.wait()
    zin = {}

    def zsend(s_from, s_to):
        dev = at_z(1 if s_to in (2, 4, 6) else -1)
        zin[s_to] = send(rg.at[s_from, core], rg.at[s_to, core], dev, "z", ("z", s_to))
        send(rg.at[s_from, core], rg.at[s_to, core], dev | pair, "x", ("x", s_to // 4))

    zsend(0, 1)
    zsend(0, 2)
    send(rg.at[0, core], rg.at[0, core], pair, "p", ("x", 0))

    diag = lax.broadcasted_iota(jnp.int32, (BR, BR), 0) == lax.broadcasted_iota(jnp.int32, (BR, BR), 1)
    lane = lax.broadcasted_iota(jnp.int32, (BR, 128), 1)
    l_lse.wait()
    turned = [
        jnp.sum(jnp.where(diag, jnp.broadcast_to(lse_v[h : h + 1, :], (BR, BR)), 0.0), axis=1, keepdims=True)
        for h in range(2)
    ]
    qol[me, :, 512:] = jnp.where(lane == 0, turned[0], turned[1])

    for c in l_w:
        c.wait()

    @pl.loop(0, WD // 32)
    def _(i):
        rows = pl.ds(pl.multiple_of(i * 32, 32), 32)
        for n in range(2):
            hi, lo = split(w2f[n, rows, :])
            w2h[rows, n * WF : (n + 1) * WF] = hi
            w2l[rows, n * WF : (n + 1) * WF] = lo

    def rows_pass(*slots):
        for s in slots:
            zin[s].wait_recv()
            if s < 6:
                zsend(s, s + 2)

    rows_pass(1, 2)
    for c in l_wd:
        c.wait()

    @pl.loop(0, WF // 128)
    def _(i):
        rows = pl.ds(pl.multiple_of(i * 128, 128), 128)
        hi, lo = split(wdf[rows, :])
        wdh[rows, :] = hi
        wdl[rows, :] = lo

    rows_pass(3)

    def split_out():
        @pl.loop(0, WD // 64)
        def _(i):
            rows = pl.ds(pl.multiple_of(i * 64, 64), 64)
            hi, lo = split(wof[rows, :])
            woh[rows, :] = hi
            wol[rows, :] = lo

    def project(k):
        both = rg[4 * k : 4 * k + 4]
        resid = both[:, :, 0].reshape(128, WD)
        grad = both[:, :, 1].reshape(128, WD)
        squares = jnp.sum(resid * resid, axis=1, keepdims=True)
        part[k, :, :, :, 2688:] = jnp.broadcast_to(squares, (128, 128)).reshape(4, 4, 8, 128)
        xh, xl = split(resid * gain[...])
        xx = jnp.concatenate([xh, xl], axis=0)
        for n in range(7):
            cols = slice(n * 256, (n + 1) * 256)
            two = nn(xx, w2h[:, cols])
            part[k, :, :, :, cols] = (two[:128] + two[128:] + nn(xh, w2l[:, cols])).reshape(4, 4, 8, 256)
        gh, gl = split(grad)
        gg = jnp.concatenate([gh, gl], axis=0)
        for lo, hi in ((0, 256), (256, 512), (512, 768), (768, 896)):
            two = nt(gg, wdh[lo:hi, :])
            part[k, :, :, :, 1792 + lo : 1792 + hi] = (
                two[:128] + two[128:] + nt(gh, wdl[lo:hi, :])
            ).reshape(4, 4, 8, hi - lo)

    axes = ((at_x, x, at_y, y), (at_y, y, at_x, x))
    cs = (slice(0, HALF), slice(HALF, WIDTH))
    LO, HI = slice(0, 640), slice(640, HALF)

    def wrap(v, o):
        return lax.rem(v + (o + 4), 4)

    VIA = {2: 1, 1: -1, 0: 1, 3: -1}

    def at_piece(k, h, r, a):
        b = wrap(axes[h][3], r)
        return (k, b, a, slice(None), cs[h]) if h == 0 else (k, a, b, slice(None), cs[h])

    m1, m2 = {}, {}

    seen = set()

    def once(key, wait):
        if key not in seen:
            seen.add(key)
            wait()

    def relay_send(k, h, r):
        go, av, _, _ = axes[h]
        m1[k, h, r] = send(
            part.at[at_piece(k, h, r, wrap(av, 2))], r1.at[k, h, r], go(VIA[r]), "rs1r", ("r", k, h, r)
        )

    def direct_send(k, h, r):
        go, av, _, _ = axes[h]
        send(part.at[at_piece(k, h, r, wrap(av, -VIA[r]))], c1.at[k, h, r, 1], go(-VIA[r]), "rs1d", ("c", k, h, r))

    def relay_add(k, h, r):
        go, av, _, _ = axes[h]
        m1[k, h, r].wait_recv()
        r1[k, h, r] = r1[k, h, r] + part[at_piece(k, h, r, wrap(av, VIA[r]))]
        send(r1.at[k, h, r], c1.at[k, h, r, 0], go(VIA[r]), "rs1c", ("c", k, h, r))

    def first_sum(k, h, r):
        _, av, go, _ = axes[h]
        arrived(("c", k, h, r), c1.at[k, h, r])
        q1[k, h, r] = part[at_piece(k, h, r, av)] + c1[k, h, r, 0] + c1[k, h, r, 1]
        if r == 2:
            for d, cols in ((1, LO), (-1, HI)):
                n = (1 - d) // 2
                m2[k, h, d] = send(
                    q1.at[k, h, 2, :, cols], r2.at[k, h, n, :, cols], go(d), "rs2", ("r2", k, h, d)
                )
        elif r == 1:
            send(q1.at[k, h, 1, :, HI], c2.at[k, h, 0, :, HI], go(1), "rs2", ("c2", k, h))
        elif r == 3:
            send(q1.at[k, h, 3, :, LO], c2.at[k, h, 1, :, LO], go(-1), "rs2", ("c2", k, h))

    def second_add(k, h, d):
        _, _, go, _ = axes[h]
        n, r, cols = (0, 1, LO) if d == 1 else (1, 3, HI)
        m2[k, h, d].wait_recv()
        r2[k, h, n, :, cols] = r2[k, h, n, :, cols] + q1[k, h, r, :, cols]
        send(r2.at[k, h, n, :, cols], c2.at[k, h, n, :, cols], go(d), "rs2", ("c2", k, h))

    def gate(k):
        sums = []
        for h in range(2):
            arrived(("c2", k, h), c2.at[k, h])
            sums.append(q1[k, h, 0] + c2[k, h, 0] + c2[k, h, 1])
        total = jnp.concatenate(sums, axis=1)
        inv = lax.rsqrt(total[:, 2688:] / D + EPS)
        inv1 = inv[:, 0:1]
        gate_raw, up_raw, d_hidden = total[:, 0:896], total[:, 896:1792], total[:, 1792:2688]
        gate_out, up_out = gate_raw * inv1, up_raw * inv1
        sig = jax.nn.sigmoid(gate_out)
        activated = gate_out * sig
        d_up = d_hidden * activated
        d_gate = d_hidden * up_out * sig * (1.0 + gate_out * (1.0 - sig))
        dot = jnp.sum(d_gate * gate_raw + d_up * up_raw, axis=1, keepdims=True)
        coef = inv * inv * inv * dot / D
        lane = lax.broadcasted_iota(jnp.int32, (8, 128), 1)
        full[k, y, x, :, 0:896] = activated * up_out
        full[k, y, x, :, 896:1792] = d_gate
        full[k, y, x, :, 1792:2688] = d_up
        full[k, y, x, :, 2688:] = jnp.where(lane < 64, inv, coef)

    def sub(c, part_of):
        return slice(c.start + part_of.start, c.start + part_of.stop)

    def fsend(k, h, r, a, dev, out, into, cols=None):
        at = at_piece(k, h, r, a)
        if cols is not None:
            at = at[:-1] + (sub(cs[h], cols),)
        return send(full.at[at], full.at[at], dev, out, into)

    g1, g2 = {}, {}

    def near(k, h, d):
        once(("b", k, h, d), g1[k, h, d].wait_recv)

    def across(k, h, r, d):
        go, av, _, _ = axes[h]
        if r == 3:
            near(k, h, 1)
        elif r == 1:
            near(k, h, -1)
        elif r == 2:
            once(("b2", k, h), lambda: arrived(("b2", k, h), q1.at[k, h, 0]))
        into = ("a", k, h, r) if d == VIA[r] else ("done", k)
        g2[k, h, r, d] = fsend(k, h, r, av, go(d), ("a", k), into)

    def own_send(k, h, d):
        _, av, go, _ = axes[h]
        g1[k, h, d] = fsend(k, h, 0, av, go(d), "ag1", ("b", k, h, d))

    def near_pass(k, h, d):
        _, av, go, _ = axes[h]
        near(k, h, d)
        fsend(k, h, 3 if d == 1 else 1, av, go(d), "ag1", ("b2", k, h), LO if d == 1 else HI)

    def across_pass(k, h, r):
        go, av, _, _ = axes[h]
        g2[k, h, r, VIA[r]].wait_recv()
        fsend(k, h, r, wrap(av, -VIA[r]), go(VIA[r]), "pass", ("done", k))

    def ag_done(k):
        arrived(("done", k), full.at[k, :, :, :, cs[0]])

    pf = {}

    def input_grad(k):
        ag_done(k)
        dgu = full[k, :, :, :, 896:2688].reshape(128, 1792)
        tile = full[k, :, :, :, 2688:].reshape(128, 128)
        inv, coef = tile[:, 0:1], tile[:, 64:65]
        dn = three(dgu, w2h[...], w2l[...], nt)
        resid = rg[4 * k : 4 * k + 4, :, 0].reshape(128, WD)
        t = dn * gain[...] * inv - resid * coef
        tpart[k] = t.reshape(4, 2, BR, WD)
        for n in (3, 2, 1, 0):
            pf[k, n] = send(tpart.at[k, n, other], tpair.at[k, n], pair, "pf", ("pf", k, n))

    def input_grad_send(k):
        for n in (3, 2, 1, 0):
            pf[k, n].wait_recv()
            usum[k, n] = tpart[k, n, core] + tpair[k, n]
            s = 4 * k + n
            if s:
                send(usum.at[k, n], rz.at[s], at_z(OFF[s]), "zf", "zf")

    def weight_grads():
        inv = full[:, :, :, :, 2688:].reshape(ROWS, 128)[:, 0:1]
        both = rg[...]
        resid = both[:, :, 0].reshape(ROWS, WD)
        grad = both[:, :, 1].reshape(ROWS, WD)
        nt_ = (resid * gain[...] * inv).T
        nh, nl = split(nt_)
        nn2 = jnp.concatenate([nh, nl], axis=0)
        for n in range(7):
            cols = slice(896 + n * 256, 896 + (n + 1) * 256)
            bh, bl = split(full[:, :, :, :, cols].reshape(ROWS, 256))
            two = nn(nn2, bh)
            gw2[:, n * 256 : (n + 1) * 256] = two[:WD] + two[WD:] + nn(nh, bl)
        gh, gl = split(grad)
        for n in range(7):
            cols = slice(n * 128, (n + 1) * 128)
            ht = full[:, :, :, :, cols].reshape(ROWS, 128).T
            hh, hl = split(ht)
            two = nn(jnp.concatenate([hh, hl], axis=0), gh)
            gwd[cols, :] = two[:128] + two[128:] + nn(hh, gl)

    def attention_split():
        for c in l_kv:
            c.wait()
        arrived("kv", kv.at[:, 0])

        @pl.loop(0, 16)
        def _(i):
            m, j = i // 8, lax.rem(i, 8)
            src = pl.ds(pl.multiple_of(j * 128, 128), 128)
            dst = pl.ds(pl.multiple_of(i * 128, 128), 128)
            for n, out in ((0, k3), (1, v3)):
                hi, lo = split(kv[n, m, src, :])
                out[dst, 0:128] = hi
                out[dst, 128:256] = lo
                out[dst, 256:384] = hi

    def attention_probs(h):
        q = qol[:, :, h * HD : (h + 1) * HD].reshape(ROWS, HD)
        lse = qol[:, :, 512:].reshape(ROWS, 128)[:, h : h + 1]
        qh, ql = split(q)
        q3 = jnp.concatenate([qh, qh, ql], axis=1)

        @pl.loop(0, 4)
        def _(i):
            keys = pl.ds(pl.multiple_of(i * 512, 512), 512)
            s = nt(q3, k3[keys, :]) * SCALE
            first = (i // 2) * (KEYS * NCTX) + me * KEYS + lax.rem(i, 2) * 512
            pos = first + lax.broadcasted_iota(jnp.int32, (ROWS, 512), 1)
            row = (CONTEXT - ROWS) + lax.broadcasted_iota(jnp.int32, (ROWS, 512), 0)
            probs[h, :, keys] = jnp.where(pos <= row, jnp.exp(s - lse), 0.0)

    def rows_pair(k):
        arrived(("x", k), rg.at[0:4, 0])

    outs = []

    def start_kv():
        send(key_h.at[0], kv.at[0, core], pair, "kv", "kv")
        send(val_h.at[0], kv.at[1, core], pair, "kv", "kv")

    def start_qo():
        for c in l_qol:
            c.wait()
        for o in ctx_offsets:
            send(qol.at[me], qol.at[me], at_ctx(*o), "qo", "qo")

    gz = {}

    def resid_own():
        total = rg[0, core, 1] + usum[0, 0]
        arrived("zf", rz.at[1:8])
        for s in range(1, 8):
            total = total + rz[s]
        gres[wide] = total
        for s in range(7, 0, -1):
            gz[s] = send(gres.at[wide], gres.at[wide], at_z(OFF[s]), "g", ("g", s))
        send(gres.at[wide], gres.at[wide], pair, "g", ("gp", 0))
        outs.append(local(gres.at[wide], gres_o))

    def resid_from(s):
        return lax.rem(z + (NZ - OFF[s]), NZ)

    def resid_pass(g):
        for s in range(max(4 * g, 1), 4 * g + 4):
            gz[s].wait_recv()
            w = 2 * resid_from(s) + core
            send(gres.at[w], gres.at[w], pair, "g", ("gp", g))
        arrived(("gp", g), gres.at[0:4])

    def d_attn_part(g):
        blocks = [2 * resid_from(s) + p for s in range(4 * g, 4 * g + 4) for p in range(2)]
        gh, gl = split(jnp.concatenate([gres[w] for w in blocks], axis=0))
        gg = jnp.concatenate([gh, gl], axis=0)
        for h in range(2):
            cols = slice(h * HD, (h + 1) * HD)
            two = nt(gg, woh[cols, :])
            out = two[:128] + two[128:] + nt(gh, wol[cols, :])
            for n, w in enumerate(blocks):
                da[h, w] = out[n * BR : (n + 1) * BR]
            for w in blocks:

                @pl.when(w != me)
                def _(w=w):
                    dev = {"y": w // NX, "x": lax.rem(w, NX)}
                    send(da.at[h, w], rda.at[h, me], dev, "di", ("di", h))

    def out_grad():
        oh, ol = split(qol[:, :, 256:512].reshape(ROWS, WD).T)
        eh, el = split(gres[...].reshape(ROWS, WD))
        two = nn(jnp.concatenate([oh, ol], axis=0), eh)
        gwo[...] = two[:WD] + two[WD:] + nn(oh, el)
        outs.append(local(gwo, gwo_o))

    def d_attn_sum(h):
        arrived(("di", h), rda.at[h, 0:15])
        own = da[h, me]
        for o in ctx_offsets:
            own = own + rda[h, ctx_of(*o)]
        dat[h, me] = own
        for o in ctx_offsets:
            send(dat.at[h, me], dat.at[h, me], at_ctx(*o), "do", ("do", h))

    def d_attn_all(h):
        arrived(("do", h), rda.at[h, 0:15])

    def query_grad(h):
        d_attn = dat[h].reshape(ROWS, HD)
        o = qol[:, :, 256 + h * HD : 256 + (h + 1) * HD].reshape(ROWS, HD)
        delta = jnp.sum(d_attn * o, axis=1, keepdims=True)
        dh, dl = split(d_attn)
        d3 = jnp.concatenate([dh, dh, dl], axis=1)
        acc[...] = jnp.zeros_like(acc)

        for i in range(4):
            keys = slice(i * 512, (i + 1) * 512)
            g = probs[h, :, keys] * (nt(d3, v3[keys, :]) - delta)
            gh, gl = split(g)
            acc[...] += nn(jnp.concatenate([gh, gl], axis=0), k3[keys, 0:256])

        a = acc[...]
        out = (a[:ROWS, :HD] + a[:ROWS, HD:] + a[ROWS:, :HD] + a[ROWS:, HD:]) * SCALE
        dq[h] = out.reshape(16, BR, HD)
        for n, o in enumerate(ctx_offsets):
            send(dq.at[h, ctx_of(*o)], rdq.at[h, n], at_ctx(*o), "qi", ("qi", h))

    def query_sum(h):
        arrived(("qi", h), rdq.at[h])
        own = dq[h, me]
        for n in range(NCTX - 1):
            own = own + rdq[h, n]
        gqs[:, h * HD : (h + 1) * HD] = own

    def store_weights():
        outs.append(local(gw2.at[:, 0:WF], gwg_o))
        outs.append(local(gw2.at[:, WF : 2 * WF], gwu_o))
        outs.append(local(gwd, gwd_o))

    def qo_wait():
        arrived("qo", qol.at[0:15])

    def finish():
        outs.append(local(gqs, gq_o))
        sixteen = full.at[0, :, :, :, cs[0]]
        for out, like in (
            ("z", rg.at[1:8, 0]), ("x", rg.at[1:8, 0]), ("p", rg.at[0, 0]), ("kv", kv.at[:, 0]), ("qo", qol.at[0:15]),
            ("rs1r", sixteen), ("rs1d", sixteen), ("rs1c", sixteen), ("rs2", q1.at[:, :, 0:3]),
            ("ag1", q1.at[:, :, 0:3]), (("a", 0), sixteen), (("a", 1), sixteen), ("pass", sixteen),
            ("pf", tpair), ("zf", rz.at[1:8]), ("g", gres.at[0:15]), ("di", rda.at[:, 0:15]), ("do", rda.at[:, 0:15]), ("qi", rdq),
        ):
            gone(out, like)
        for c in outs:
            c.wait()

    def enter(k):
        rows_pair(k)
        project(k)
        if k == 1:
            start_kv()

    steps = {
        "S": relay_send, "D": direct_send, "R": relay_add, "F": first_sum, "T": second_add, "G": gate,
        "O": own_send, "A": across, "N": near_pass, "P": across_pass, "Z": rows_pass, "J": enter,
    }
    enter(0)
    for step in ORDER:
        steps[step[0]](*step[1:])
    input_grad(0)
    input_grad_send(0)
    input_grad(1)
    input_grad_send(1)
    start_qo()
    weight_grads()
    store_weights()
    attention_split()
    split_out()
    resid_own()
    resid_pass(0)
    d_attn_part(0)
    resid_pass(1)
    d_attn_part(1)
    qo_wait()
    out_grad()
    attention_probs(0)
    d_attn_sum(0)
    d_attn_sum(1)
    attention_probs(1)
    d_attn_all(0)
    query_grad(0)
    d_attn_all(1)
    query_grad(1)
    query_sum(0)
    query_sum(1)
    finish()


def put(*refs):
    sem = refs[12]
    copies = [pltpu.make_async_copy(refs[n], refs[6 + n], sem.at[n]) for n in range(6)]
    for c in copies:
        c.start()
    for c in copies:
        c.wait()


def shards(residual, grad_out, norm_gain, w_gate, w_up, w_down, w_out, queries, attn_out, log_sum_exp, key_cache, value_cache):
    operands = (
        residual, grad_out, norm_gain.reshape(1, WD), w_gate, w_up, w_down, w_out,
        queries, attn_out, log_sum_exp, key_cache, value_cache,
    )
    V = pltpu.VMEM
    shape = jax.ShapeDtypeStruct
    scratch = [
        V((8, 2, 2, BR, WD), F32),
        V((1, WD), F32), V((2, BR), F32),
        V((2, WD, WF), F32), V((WF, WD), F32), V((WD, WD), F32),
        V((WD, 2 * WF), BF16), V((WD, 2 * WF), BF16),
        V((WF, WD), BF16), V((WF, WD), BF16),
        V((WD, WD), BF16), V((WD, WD), BF16),
        V((16, BR, 640), F32),
        V((2, 2, KEYS, HD), F32),
        V((2 * KEYS, 384), BF16), V((2 * KEYS, 384), BF16),
        V((2, 4, 4, 8, WIDTH), F32),
        V((2, 2, 4, 8, HALF), F32), V((2, 2, 4, 2, 8, HALF), F32),
        V((2, 2, 4, 8, HALF), F32),
        V((2, 2, 2, 8, HALF), F32), V((2, 2, 2, 8, HALF), F32),
        V((2, 4, 4, 8, WIDTH), F32),
        V((2, 4, 2, BR, WD), F32), V((2, 4, BR, WD), F32), V((2, 4, BR, WD), F32),
        V((8, BR, WD), F32),
        V((16, BR, WD), F32), V((2, 16, BR, HD), F32), V((2, 16, BR, HD), F32), V((2, 16, BR, HD), F32),
        V((2, ROWS, 2 * KEYS), F32),
        V((2 * ROWS, 2 * HD), F32),
        V((2, 16, BR, HD), F32), V((2, 15, BR, HD), F32),
        V((WD, 2 * WF), F32), V((WF, WD), F32), V((WD, WD), F32), V((BR, WD), F32),
        pltpu.SemaphoreType.DMA((18,)),
        pltpu.SemaphoreType.DMA((19,)),
        pltpu.SemaphoreType.DMA((NSEM,)),
    ]
    hbm = pl.BlockSpec(memory_space=pltpu.HBM)
    anyspec = pl.BlockSpec(memory_space=pl.ANY)
    sent = pl.pallas_call(
        kernel,
        out_shape=(
            shape((WD, WF), F32), shape((WD, WF), F32), shape((WF, WD), F32),
            shape((WD, WD), F32), shape((BR, WD), F32), shape((BR, WD), F32),
        ),
        in_specs=[hbm] * 12,
        out_specs=(anyspec,) * 6,
        scratch_shapes=scratch,
        compiler_params=pltpu.CompilerParams(
            collective_id=0, has_side_effects=True, vmem_limit_bytes=LIMIT
        ),
    )(*[pltpu.with_memory_space_constraint(a, pltpu.HBM) for a in operands])
    return pl.pallas_call(
        put,
        out_shape=tuple(shape(o.shape, F32) for o in sent),
        in_specs=[anyspec] * 6,
        out_specs=(hbm,) * 6,
        scratch_shapes=[pltpu.SemaphoreType.DMA((6,))],
        compiler_params=pltpu.CompilerParams(vmem_limit_bytes=1024 * 1024),
    )(*sent)


def solution(mesh):
    torus = Mesh(mesh.devices.reshape(NZ, 2, NY, NX), ("z", "core", "y", "x"))
    wide, ctx = ("z", "core"), ("y", "x")
    return jax.shard_map(
        shards,
        mesh=torus,
        in_specs=(
            P(wide, ctx), P(wide, ctx), P(ctx), P(ctx, wide), P(ctx, wide), P(wide, ctx), P(wide, ctx),
            P(ctx, wide), P(ctx, wide), P(wide, ctx), P(wide, ctx, None), P(wide, ctx, None),
        ),
        out_specs=(P(ctx, wide), P(ctx, wide), P(wide, ctx), P(wide, ctx), P(wide, ctx), P(ctx, wide)),
        check_vma=False,
    )
```
